32 devices in a mesh: dp: 2 (over y), expert: 16 (over z, x, core).
Axes of the slice: x: 2, y: 2, z: 4, core: 2. Of those that a mesh axis runs over, the one named last changes fastest.
Arguments:
- tokens_in: bfloat16 [32, 512, 1536], P('expert', 'dp'), may hold values from -6 to 6
- out_grad: bfloat16 [32, 512, 1536], P('expert', 'dp'), may hold values from -6 to 6
- seq_lengths: int32 [32], P('expert'), may hold values from 1 to 512, 12288 in all
- seq_order: int32 [32], P('expert'), may hold values from 0 to 1, as said below
- routes_top: int32 [32, 512, 6], P(('dp', 'expert')), may hold values from 0 to 15, all different within a row; in each aligned block of 512 rows (0 to 511, 512 to 1023, ..., all dimensions but the last counted through in order) at most 216 rows name the same one
- norm_gain: float32 [1536], P(('dp', 'expert')), may hold values from 0.5 to 1.5
- in_weight: float32 [1536, 6448], P(('dp', 'expert')), may hold values from -0.15625 to 0.15625
- conv_weight: float32 [3328, 4], P(('dp', 'expert')), may hold values from -3 to 3
- conv_bias: float32 [3328], P(('dp', 'expert')), may hold values from -1.8 to 1.8
- step_bias: float32 [48], replicated, may hold values from -5 to -1
- decay_log: float32 [48], replicated, may hold values from 0 to 2.7
- skip_gain: float32 [48], replicated, may hold values from 0.5 to 1.5
- gated_gain: float32 [3072], P(('dp', 'expert')), may hold values from 0.5 to 1.5
- out_weight: float32 [3072, 1536], P(('dp', 'expert')), may hold values from -0.109375 to 0.109375
- ffn_gain: float32 [1536], P(('dp', 'expert')), may hold values from 0.5 to 1.5
- router_weight: float32 [1536, 16], P(('dp', 'expert')), may hold values from -0.078125 to 0.078125
- expert_gate_up: float32 [16, 1536, 1024], P('expert', 'dp'), may hold values from -0.15625 to 0.15625
- expert_down: float32 [16, 512, 1536], P('expert', 'dp'), may hold values from -0.5 to 0.5
- shared_gate_up: float32 [1536, 2048], P(('dp', 'expert')), may hold values from -0.15625 to 0.15625
- shared_down: float32 [1024, 1536], P(('dp', 'expert')), may hold values from -0.375 to 0.375
Outputs:
- block_out: bfloat16 [32, 512, 1536], P('expert', 'dp')
- input_grad: bfloat16 [32, 512, 1536], P('expert', 'dp')
- grad_norm_gain: float32 [1536], P(('dp', 'expert'))
- grad_in_weight: float32 [1536, 6448], P(('dp', 'expert'))
- grad_conv_weight: float32 [3328, 4], P(('dp', 'expert'))
- grad_conv_bias: float32 [3328], P(('dp', 'expert'))
- grad_step_bias: float32 [48], replicated
- grad_decay_log: float32 [48], replicated
- grad_skip_gain: float32 [48], replicated
- grad_gated_gain: float32 [3072], P(('dp', 'expert'))
- grad_out_weight: float32 [3072, 1536], P(('dp', 'expert'))
- grad_ffn_gain: float32 [1536], P(('dp', 'expert'))
- grad_router_weight: float32 [1536, 16], P(('dp', 'expert'))
- grad_expert_gate_up: float32 [16, 1536, 1024], P('expert', 'dp')
- grad_expert_down: float32 [16, 512, 1536], P('expert', 'dp')
- grad_shared_gate_up: float32 [1536, 2048], P(('dp', 'expert'))
- grad_shared_down: float32 [1024, 1536], P(('dp', 'expert'))
The draws below stay inside these ranges and needn't reach their ends.
Inputs may be any that keep to these rules, and one draw needn't show every extreme that they name: `routes_top`: each row names 6 different experts; among the rows of one device's tile no expert is named more than 216 times, a bound that some block reaches. `seq_lengths`: some sequence is exactly 512 long. `seq_order`: each aligned group of 2 entries (the sequences of one index of expert) is a permutation of 0 to 1.
All inputs are finite; a program needn't handle non-finite values. No bound on the sum of `seq_lengths` on one device may be relied on, other than what follows from the above.
Results may differ from the reference program's by a relative error of at most 0.012.
The reference program's roundings to bfloat16 on the way count: a program that leaves them out, or rounds other values in their place, can miss the bound.
Values may be sent and summed in bfloat16 or wider, within the bound.
No kernel may reach another device: no remote copies, remote signals or barrier semaphores. Data moves between devices by JAX's collectives and lax.ppermute only.
A program may use at most 576 MiB of HBM per device.

```python
import math
import jax
import jax.numpy as jnp
import numpy as np
from jax import lax

D = 1536
HEADS = 48
CONV_WIDTH = 4
EXPERT_FF = 512
SHARED_FF = 1024
TOPK = 6
BLK = 128
LEN = 512
INNER = 3072
CONV_DIM = 3328
PROJ = 6448
EXPERTS = 16
SEQS = 32
CAP = 216
N_DP = 2
N_EXPERT = 16


def draw_seq_order(key, part):
    groups = SEQS // N_DP
    scores = jax.random.randint(key, (groups, N_DP), 0, 1 << 20) * N_DP + lax.broadcasted_iota(jnp.int32, (groups, N_DP), 1)
    ranks = jnp.sum((scores[:, None, :] < scores[:, :, None]).astype(jnp.int32), axis=2)
    return ranks.reshape(SEQS).astype(jnp.int32)


def level_of(own_key, extent, pieces, low, largest):
    loudness = 1.0
    for position, shards_of in pieces:
        steps = jax.random.uniform(jax.random.fold_in(jax.random.fold_in(own_key, 6), position), (shards_of,), jnp.float32, low / len(pieces), largest / len(pieces))
        loudness = loudness * jnp.repeat(jnp.exp(steps), extent[position] // shards_of).reshape((-1,) + (1,) * (len(extent) - 1 - position))
    return loudness


def split_up(number_of, total, bound, slope):
    portions = [(1 << 20) // math.isqrt(grade ** slope) + 1 for grade in range(2, number_of + 1)]
    rest, counts = total - bound - (number_of - 1), [1] * (number_of - 1)
    while rest > 0:
        candidates = [i for i in range(number_of - 1) if counts[i] < bound]
        whole, remaining = sum([portions[i] for i in candidates]), rest
        for i in candidates:
            more = min(bound - counts[i], max(1, remaining * portions[i] // whole), rest)
            counts[i] = counts[i] + more
            rest = rest - more
    return np.array([bound] + counts)


def uneven(own_key, number_of, total, bound, slope):
    if number_of == 2:
        one = jax.random.randint(own_key, (), max(1, total - bound), min(bound, total - 1) + 1)
        return jnp.stack([one, total - one])
    sizes = jnp.asarray(split_up(number_of, total, bound, slope), jnp.int32)
    pairs = (number_of - 1) // 2
    donor, receiver = sizes[1:1 + 2 * pairs:2], sizes[2:2 + 2 * pairs:2]
    slack = jnp.minimum(donor - 1, bound - receiver)
    passed = jax.random.randint(jax.random.fold_in(own_key, 1), (pairs,), 0, 1 << 20) % (slack + 1)
    sizes = sizes.at[1:1 + 2 * pairs:2].set(donor - passed).at[2:2 + 2 * pairs:2].set(receiver + passed)
    return sizes[jax.random.permutation(jax.random.fold_in(own_key, 2), number_of)]


def assign_block(stream_key, own, number, rows, number_of, top, reach, slope):
    sequence = jax.random.permutation(stream_key, number_of)
    crowded, usual = portions_of(number_of, rows * top, reach, slope, True), portions_of(number_of, rows * top, reach, slope, False)
    places = jnp.arange(number_of)

    def named(sizes, offset_by):
        used = int((sizes > 0).sum())
        fixed = max(1, used // 4)
        moved = fixed + (places - fixed + offset_by * (used - fixed)) % max(1, number_of - fixed)
        return jnp.zeros((number_of,), jnp.int32).at[sequence[jnp.where(places < fixed, places, moved)]].set(jnp.asarray(sizes, jnp.int32))

    sizes = jnp.where(number % 4 == 0, named(crowded, number // 4), named(usual, number - number // 4 - 1))
    mixed = jax.random.permutation(jax.random.fold_in(own, 3), number_of)
    donor, receiver = mixed[0:number_of // 2 * 2:2], mixed[1:number_of // 2 * 2:2]
    slack = jnp.minimum(sizes[donor] - 1, reach - sizes[receiver]) // 2
    slack = jnp.where((donor == sequence[0]) | (receiver == sequence[0]) | (sizes[receiver] == 0), 0, jnp.maximum(slack, 0))
    moved = jax.random.randint(jax.random.fold_in(own, 4), (number_of // 2,), 0, 1 << 20) % (slack + 1)
    sizes = sizes.at[donor].add(-moved).at[receiver].add(moved)
    labels = jnp.searchsorted(jnp.cumsum(sizes), jnp.arange(rows * top), side="right").astype(jnp.int32)
    listing = labels.reshape(top, rows).T
    listing = listing[jax.random.permutation(jax.random.fold_in(own, 1), rows)]
    offset_by = jax.random.randint(jax.random.fold_in(own, 2), (rows, 1), 0, top)
    return jnp.take_along_axis(listing, (jnp.arange(top)[None, :] + offset_by) % top, axis=1)


def portions_of(amount, total, limit, slope, full):
    loads = [(1 << 20) // math.isqrt(standing ** slope) + 1 for standing in range(1, amount + 1)]
    largest = limit if full else min(limit, max(-(-total // amount), total * loads[0] // sum(loads)))
    least = 1 if total - largest >= amount - 1 else 0
    holding, surplus = [largest] + [least] * (amount - 1), total - largest - least * (amount - 1)
    while surplus > 0:
        candidates = [i for i in range(1, amount) if holding[i] < largest] or [i for i in range(1, amount) if holding[i] < limit]
        pool, remaining = sum([loads[i] for i in candidates]), surplus
        for i in candidates:
            addition = min(limit - holding[i], max(1, remaining * loads[i] // pool), surplus)
            holding[i] = holding[i] + addition
            surplus = surplus - addition
    return np.array(holding)


def bell_draw(own_key, dims, deviation, most, pieces=(), dtype=jnp.bfloat16):
    level = level_of(own_key, dims, pieces, -0.22, 0.18) if pieces else 1.0
    drawn = jax.random.normal(own_key, dims, jnp.float32) * deviation * level
    return jnp.minimum(jnp.maximum(drawn, -most), most).astype(dtype)


def setup_inputs(seed: int = 0) -> dict:
    key_list = jax.random.split(jax.random.key(seed), 21)
    tokens_in = bell_draw(key_list[0], (SEQS, LEN, D), 1.0, 6.0, ((0, 16), (1, 2)))
    out_grad = bell_draw(key_list[1], (SEQS, LEN, D), 1.0, 6.0, ((0, 16), (1, 2)))
    seq_lengths = uneven(key_list[2], SEQS, SEQS * LEN * 3 // 4, LEN, 1).astype(jnp.int32)
    seq_order = draw_seq_order(jax.random.fold_in(key_list[20], 71), 0)
    routes_top_keys = jax.random.split(jax.random.fold_in(key_list[4], 1), SEQS * LEN // LEN)
    routes_top_turns = jax.random.permutation(jax.random.fold_in(key_list[4], 3), SEQS * LEN // LEN)
    routes_top = jax.vmap(lambda own, number: assign_block(jax.random.fold_in(key_list[4], 2), own, number, LEN, EXPERTS, TOPK, CAP, 1))(routes_top_keys, routes_top_turns).reshape((SEQS, LEN, TOPK))
    norm_gain = jnp.clip(1.0 + 0.1 * jax.random.normal(key_list[5], (D,), jnp.float32), 0.5, 1.5)
    in_weight = bell_draw(key_list[6], (D, PROJ), D ** -0.5, 0.15625, ((0, 32),), jnp.float32)
    conv_weight = bell_draw(key_list[7], (CONV_DIM, CONV_WIDTH), CONV_WIDTH ** -0.5, 3.0, ((0, 32),), jnp.float32)
    conv_bias = bell_draw(key_list[8], (CONV_DIM,), 0.3, 1.8, ((0, 32),), jnp.float32)
    step_bias = jnp.clip(jax.random.uniform(key_list[9], (HEADS,), jnp.float32, -5.0, -1.0), -5.0, -1.0)
    decay_log = jnp.clip(jax.random.uniform(key_list[10], (HEADS,), jnp.float32, 0.0, 2.7), 0.0, 2.7)
    skip_gain = jnp.clip(jax.random.uniform(key_list[11], (HEADS,), jnp.float32, 0.5, 1.5), 0.5, 1.5)
    gated_gain = jnp.clip(1.0 + 0.1 * jax.random.normal(key_list[12], (INNER,), jnp.float32), 0.5, 1.5)
    out_weight = bell_draw(key_list[13], (INNER, D), INNER ** -0.5, 0.109375, ((0, 32),), jnp.float32)
    ffn_gain = jnp.clip(1.0 + 0.1 * jax.random.normal(key_list[14], (D,), jnp.float32), 0.5, 1.5)
    router_weight = bell_draw(key_list[15], (D, EXPERTS), (4 * D) ** -0.5, 0.078125, ((0, 32),), jnp.float32)
    expert_gate_up = bell_draw(key_list[16], (EXPERTS, D, 2 * EXPERT_FF), D ** -0.5, 0.15625, ((0, 16), (1, 2)), jnp.float32)
    expert_down = bell_draw(key_list[17], (EXPERTS, EXPERT_FF, D), (EXPERT_FF // 4) ** -0.5, 0.5, ((0, 16), (1, 2)), jnp.float32)
    shared_gate_up = bell_draw(key_list[18], (D, 2 * SHARED_FF), D ** -0.5, 0.15625, ((0, 32),), jnp.float32)
    shared_down = bell_draw(key_list[19], (SHARED_FF, D), (SHARED_FF // 4) ** -0.5, 0.375, ((0, 32),), jnp.float32)
    return {"tokens_in": tokens_in, "out_grad": out_grad, "seq_lengths": seq_lengths, "seq_order": seq_order, "routes_top": routes_top, "norm_gain": norm_gain, "in_weight": in_weight, "conv_weight": conv_weight, "conv_bias": conv_bias, "step_bias": step_bias, "decay_log": decay_log, "skip_gain": skip_gain, "gated_gain": gated_gain, "out_weight": out_weight, "ffn_gain": ffn_gain, "router_weight": router_weight, "expert_gate_up": expert_gate_up, "expert_down": expert_down, "shared_gate_up": shared_gate_up, "shared_down": shared_down}


@jax.custom_vjp
def low(v):
    return lax.optimization_barrier(v.astype(jnp.bfloat16)).astype(jnp.float32)

@jax.custom_vjp
def low_back(v):
    return v

def low_keep(v):
    return (low(v), None)

def low_pass(kept, grad):
    return (grad,)

def back_keep(v):
    return (v, None)

def back_low(kept, grad):
    return (low(grad),)
low.defvjp(low_keep, low_pass)
low_back.defvjp(back_keep, back_low)
EPSILON = 1e-05
FULL_PRECISION = lax.Precision.HIGHEST

def rms_scale(values, gain_row):
    return values * lax.rsqrt(lax.optimization_barrier(jnp.mean(values * values, axis=-1, keepdims=True)) + EPSILON) * gain_row

def swiglu(pre_act):
    half_width = pre_act.shape[-1] // 2
    return jax.nn.silu(pre_act[..., :half_width]) * pre_act[..., half_width:]

def matmul(left_mat, right_mat):
    return jnp.dot(left_mat, right_mat, precision=FULL_PRECISION, preferred_element_type=jnp.float32)

def ssd_blocks(head_inputs, step_sizes, decay_rates, state_in, state_out, block_len):
    seq_count, length, head_count, head_width = head_inputs.shape
    blocks = length // block_len
    head_inputs = head_inputs.reshape(seq_count, blocks, block_len, head_count, head_width)
    step_sizes = step_sizes.reshape(seq_count, blocks, block_len, head_count)
    state_in = state_in.reshape(seq_count, blocks, block_len, -1)
    state_out = state_out.reshape(seq_count, blocks, block_len, -1)
    log_decay = step_sizes * -jnp.exp(decay_rates)
    running = jnp.cumsum(log_decay, axis=2)
    spread = running[:, :, :, None, :] - running[:, :, None, :, :]
    causal = (lax.broadcasted_iota(jnp.int32, (block_len, block_len), 0) >= lax.broadcasted_iota(jnp.int32, (block_len, block_len), 1))[None, None, :, :, None]
    decay_mat = jnp.where(causal, jnp.exp(jnp.where(causal, spread, 0.0)), 0.0)
    scores = jnp.einsum('sktn,skjn->sktj', state_out, state_in, precision=FULL_PRECISION)
    mixing = scores[..., None] * decay_mat * step_sizes[:, :, None, :, :]
    inside = jnp.einsum('sktjh,skjhp->skthp', mixing, head_inputs, precision=FULL_PRECISION)
    tail_decay = jnp.exp(running[:, :, -1:, :] - running) * step_sizes
    states = jnp.einsum('skjh,skjhp,skjn->skhpn', tail_decay, head_inputs, state_in, precision=FULL_PRECISION)
    totals = jnp.exp(running[:, :, -1, :])

    def carry_step(previous, carried):
        block_state, factor = carried
        return (previous * factor[:, :, None, None] + block_state, previous)
    initial = jnp.zeros((seq_count, head_count, head_width, state_in.shape[-1]), jnp.float32)
    _, before = lax.scan(carry_step, initial, (jnp.moveaxis(states, 1, 0), jnp.moveaxis(totals, 1, 0)))
    before = jnp.moveaxis(before, 0, 1)
    across = jnp.einsum('sktn,skhpn->skthp', state_out, before, precision=FULL_PRECISION) * jnp.exp(running)[..., None]
    return (inside + across).reshape(seq_count, length, head_count, head_width)

def mixer_local(projected, conv_kernel, conv_shift, step_shift, decay_rates, skip_weights, gated_scale, seq_count, block_len):
    inner_width = gated_scale.shape[0]
    head_count = decay_rates.shape[0]
    total_rows, proj_width = projected.shape
    length = total_rows // seq_count
    gate_part = projected[:, :inner_width]
    conv_input = projected[:, inner_width:proj_width - head_count].reshape(seq_count, length, -1)
    step_raw = projected[:, proj_width - head_count:]
    kernel_len = conv_kernel.shape[1]
    padded = jnp.pad(conv_input, ((0, 0), (kernel_len - 1, 0), (0, 0)))
    convolved = conv_shift
    for offset in range(kernel_len):
        convolved = convolved + conv_kernel[:, offset] * padded[:, offset:offset + length]
    convolved = jax.nn.silu(convolved)
    state_width = (convolved.shape[-1] - inner_width) // 2
    head_inputs = convolved[..., :inner_width].reshape(seq_count, length, head_count, inner_width // head_count)
    state_in = convolved[..., inner_width:inner_width + state_width]
    state_out = convolved[..., inner_width + state_width:]
    step_sizes = jax.nn.softplus(step_raw + step_shift).reshape(seq_count, length, head_count)
    scanned = ssd_blocks(head_inputs, step_sizes, decay_rates, state_in, state_out, block_len)
    scanned = scanned + skip_weights[:, None] * head_inputs
    gated_in = scanned.reshape(total_rows, inner_width) * jax.nn.silu(gate_part)
    return rms_scale(gated_in, gated_scale)

def block_forward(tokens, params, valid_rows, routes, seq_count):
    norm_gain, in_weight, conv_weight, conv_bias, step_bias, decay_log, skip_gain, gated_gain, out_weight, ffn_gain, router_weight, expert_gate_up, expert_down, shared_gate_up, shared_down = params
    flat_in = tokens.reshape(-1, tokens.shape[-1])
    normed = low(rms_scale(flat_in, low(norm_gain)))
    projected = low_back(matmul(normed, low(in_weight)))
    gated_out = low(mixer_local(projected, low(conv_weight), low(conv_bias), step_bias, decay_log, skip_gain, low(gated_gain), seq_count, BLK))
    middle = flat_in + low_back(matmul(gated_out, low(out_weight)))
    normed_two = low(rms_scale(middle, low(ffn_gain)))
    logits = low_back(matmul(normed_two, low(router_weight)))
    gate_weights = jax.nn.softmax(jnp.take_along_axis(logits, routes, axis=1), axis=-1)
    expert_ids = lax.broadcasted_iota(jnp.int32, (1, 1, logits.shape[1]), 2)
    combine = lax.optimization_barrier(jnp.sum(jnp.where(routes[:, :, None] == expert_ids, gate_weights[:, :, None], 0.0), axis=1))
    shared_act = low(swiglu(low_back(matmul(normed_two, low(shared_gate_up)))))
    shared_out = low_back(matmul(shared_act, low(shared_down)))

    def one_expert(running_sum, carried):
        weight_up, weight_down, column = carried
        inputs = low_back(normed_two)
        expert_act = low(swiglu(low_back(matmul(inputs, low(weight_up)))))
        result = low_back(low(matmul(expert_act, low(weight_down))))
        return (running_sum + column[:, None] * result, None)
    mixture, _ = lax.scan(jax.checkpoint(one_expert), jnp.zeros_like(middle), (expert_gate_up, expert_down, combine.T))
    return valid_rows * (middle + mixture + shared_out)

def reference(tokens_in, out_grad, seq_lengths, seq_order, routes_top, norm_gain, in_weight, conv_weight, conv_bias, step_bias, decay_log, skip_gain, gated_gain, out_weight, ffn_gain, router_weight, expert_gate_up, expert_down, shared_gate_up, shared_down):
    params = (norm_gain, in_weight, conv_weight, conv_bias, step_bias, decay_log, skip_gain, gated_gain, out_weight, ffn_gain, router_weight, expert_gate_up, expert_down, shared_gate_up, shared_down)
    group_size = math.gcd(SEQS, max(1, 4096 // LEN))
    group_count = SEQS // group_size
    seq_ids = lax.iota(jnp.int32, SEQS)
    device_of = (seq_order * N_EXPERT + seq_ids // N_DP).astype(jnp.int32)
    route_seq = jnp.take(routes_top, device_of, axis=0)
    valid_all = (lax.broadcasted_iota(jnp.int32, (SEQS, LEN), 1) < seq_lengths[:, None]).astype(jnp.float32)
    tokens_all = tokens_in.astype(jnp.float32).reshape(group_count, group_size, LEN, D)
    cot_all = out_grad.astype(jnp.float32).reshape(group_count, group_size * LEN, D)
    valid_blocks = valid_all.reshape(group_count, group_size * LEN, 1)
    route_blocks = route_seq.reshape(group_count, group_size * LEN, TOPK)

    def one_group(totals, carried):
        tokens, cotangent, valid_rows, routes = carried

        def forward(tok_values, param_values):
            return block_forward(tok_values, param_values, valid_rows, routes, group_size)
        result, backward = jax.vjp(forward, tokens, params)
        token_grad, param_grads = backward(cotangent)
        return (jax.tree.map(jnp.add, totals, param_grads), (result, token_grad))
    zero_grads = jax.tree.map(jnp.zeros_like, params)
    totals, (outputs, token_grads) = lax.scan(one_group, zero_grads, (tokens_all, cot_all, valid_blocks, route_blocks))
    block_out = outputs.reshape(SEQS, LEN, D).astype(jnp.bfloat16)
    input_grad = token_grads.reshape(SEQS, LEN, D).astype(jnp.bfloat16)
    return (block_out, input_grad, totals[0], totals[1], totals[2], totals[3], totals[4], totals[5], totals[6], totals[7], totals[8], totals[9], totals[10], totals[11], totals[12], totals[13], totals[14])
```

```python
from functools import partial
import math

import jax
import jax.numpy as jnp
from jax import lax
from jax.sharding import Mesh, PartitionSpec as P

BLK = 128
EPSILON = 1e-05
FULL_PRECISION = lax.Precision.HIGHEST
SPLIT = ("e3", "e2", "e1", "e0")
EVERY = ("dp",) + SPLIT
GROUP = SPLIT[1:]
HOLDERS = ("e3", "dp")


def rms_scale(values, gain_row):
    return (
        values * lax.rsqrt(jnp.mean(values * values, axis=-1, keepdims=True) + EPSILON) * gain_row
    )


def swiglu(pre_act):
    half_width = pre_act.shape[-1] // 2
    return jax.nn.silu(pre_act[..., :half_width]) * pre_act[..., half_width:]


def ssd_blocks(head_inputs, step_sizes, decay_rates, state_in, state_out, block_len):
    seq_count, length, head_count, head_width = head_inputs.shape
    blocks = length // block_len
    head_inputs = head_inputs.reshape(seq_count, blocks, block_len, head_count, head_width)
    step_sizes = step_sizes.reshape(seq_count, blocks, block_len, head_count)
    state_in = state_in.reshape(seq_count, blocks, block_len, -1)
    state_out = state_out.reshape(seq_count, blocks, block_len, -1)
    log_decay = step_sizes * -jnp.exp(decay_rates)
    running = jnp.cumsum(log_decay, axis=2)
    spread = running[:, :, :, None, :] - running[:, :, None, :, :]
    causal = (
        lax.broadcasted_iota(jnp.int32, (block_len, block_len), 0)
        >= lax.broadcasted_iota(jnp.int32, (block_len, block_len), 1)
    )[None, None, :, :, None]
    decay_mat = jnp.where(causal, jnp.exp(jnp.where(causal, spread, 0.0)), 0.0)
    scores = jnp.einsum("sktn,skjn->sktj", state_out, state_in, precision=FULL_PRECISION)
    mixing = scores[..., None] * decay_mat * step_sizes[:, :, None, :, :]
    inside = jnp.einsum("sktjh,skjhp->skthp", mixing, head_inputs, precision=FULL_PRECISION)
    tail_decay = jnp.exp(running[:, :, -1:, :] - running) * step_sizes
    states = jnp.einsum(
        "skjh,skjhp,skjn->skhpn", tail_decay, head_inputs, state_in, precision=FULL_PRECISION
    )
    totals = jnp.exp(running[:, :, -1, :])

    def carry_step(previous, carried):
        block_state, factor = carried
        return (previous * factor[:, :, None, None] + block_state, previous)

    initial = jnp.zeros((seq_count, head_count, head_width, state_in.shape[-1]), jnp.float32)
    _, before = lax.scan(
        carry_step, initial, (jnp.moveaxis(states, 1, 0), jnp.moveaxis(totals, 1, 0))
    )
    before = jnp.moveaxis(before, 0, 1)
    across = (
        jnp.einsum("sktn,skhpn->skthp", state_out, before, precision=FULL_PRECISION)
        * jnp.exp(running)[..., None]
    )
    return (inside + across).reshape(seq_count, length, head_count, head_width)


def mixer_local(
    projected,
    conv_kernel,
    conv_shift,
    step_shift,
    decay_rates,
    skip_weights,
    gated_scale,
    seq_count,
    block_len,
):
    inner_width = gated_scale.shape[0]
    head_count = decay_rates.shape[0]
    total_rows, proj_width = projected.shape
    length = total_rows // seq_count
    gate_part = projected[:, :inner_width]
    conv_input = projected[:, inner_width : proj_width - head_count].reshape(seq_count, length, -1)
    step_raw = projected[:, proj_width - head_count :]
    kernel_len = conv_kernel.shape[1]
    padded = jnp.pad(conv_input, ((0, 0), (kernel_len - 1, 0), (0, 0)))
    convolved = conv_shift
    for offset in range(kernel_len):
        convolved = convolved + conv_kernel[:, offset] * padded[:, offset : offset + length]
    convolved = jax.nn.silu(convolved)
    state_width = (convolved.shape[-1] - inner_width) // 2
    head_inputs = convolved[..., :inner_width].reshape(
        seq_count, length, head_count, inner_width // head_count
    )
    state_in = convolved[..., inner_width : inner_width + state_width]
    state_out = convolved[..., inner_width + state_width :]
    step_sizes = jax.nn.softplus(step_raw + step_shift).reshape(seq_count, length, head_count)
    scanned = ssd_blocks(head_inputs, step_sizes, decay_rates, state_in, state_out, block_len)
    scanned = scanned + skip_weights[:, None] * head_inputs
    gated_in = scanned.reshape(total_rows, inner_width) * jax.nn.silu(gate_part)
    return rms_scale(gated_in, gated_scale)


def dot_right(left_mat, right_mat):
    return lax.dot_general(
        left_mat, right_mat, (((1,), (1,)), ((), ())), preferred_element_type=jnp.float32
    )


def dot_left(left_mat, right_mat):
    return lax.dot_general(
        left_mat, right_mat, (((0,), (0,)), ((), ())), preferred_element_type=jnp.float32
    )


def to_low(weight):
    return weight.astype(jnp.bfloat16)


def gather_rows(block, axes):
    return lax.all_gather(block, axes, axis=0, tiled=True)


def scatter_rows(block, axes):
    return lax.psum_scatter(block, axes, scatter_dimension=0, tiled=True)


def dot(left_mat, right_mat):
    return jnp.dot(left_mat, right_mat, preferred_element_type=jnp.float32)


def local(
    tokens_in,
    out_grad,
    seq_lengths,
    seq_order,
    routes_top,
    norm_gain,
    in_weight,
    conv_weight,
    conv_bias,
    step_bias,
    decay_log,
    skip_gain,
    gated_gain,
    out_weight,
    ffn_gain,
    router_weight,
    expert_gate_up,
    expert_down,
    shared_gate_up,
    shared_down,
):
    group_count = lax.axis_size("dp")
    my_rank = lax.axis_index("dp")
    peers = lax.axis_size(GROUP)
    halves = lax.axis_size("e3")
    device_total = lax.axis_size(EVERY)

    small = [norm_gain, conv_weight, conv_bias, gated_gain, ffn_gain, router_weight]
    small_flat = jnp.concatenate([to_low(v).reshape(1, -1) for v in small], axis=1)
    small_all = gather_rows(small_flat, EVERY)
    smalls = []
    offset = 0
    for v in small:
        smalls.append(
            small_all[:, offset : offset + v.size].reshape((device_total * v.shape[0],) + v.shape[1:])
        )
        offset += v.size
    gain_one, kernel_low, shift_low, gated_scale_low, gain_two, w_router = smalls

    slot_rows = lax.broadcasted_iota(jnp.int32, (group_count, group_count), 0)
    slot_cols = lax.broadcasted_iota(jnp.int32, (group_count, group_count), 1)
    picks = (seq_order[None, :] == slot_rows).astype(jnp.int32)
    inverse = jnp.sum(picks * slot_cols, axis=1)
    my_length = jnp.sum(jnp.where(seq_order == my_rank, seq_lengths, 0))
    dealt_in, dealt_grad = (
        lax.all_to_all(
            jnp.take(tokens_in, inverse, axis=0), "dp", split_axis=0, concat_axis=1, tiled=True
        ),
        lax.all_to_all(
            jnp.take(out_grad, inverse, axis=0), "dp", split_axis=0, concat_axis=1, tiled=True
        ),
    )
    seq_count, length, model_width = dealt_in.shape
    row_count = seq_count * length
    top_count = routes_top.shape[2]
    expert_count = w_router.shape[1]
    positions = lax.broadcasted_iota(jnp.int32, (row_count, 1), 0)
    valid = positions < my_length
    valid_rows = valid.astype(jnp.float32)
    cot_low = jnp.where(valid, dealt_grad.reshape(row_count, model_width), 0)
    row_cot = cot_low.astype(jnp.float32)

    w_in = gather_rows(to_low(in_weight), EVERY)

    routes = routes_top.reshape(row_count, top_count)
    expert_ids = lax.broadcasted_iota(jnp.int32, (1, expert_count), 1)
    chosen = jnp.any(routes[:, :, None] == expert_ids[:, None, :], axis=1)
    routes_all = gather_rows(jnp.where(valid, routes, -1), GROUP).reshape(
        peers, row_count, top_count
    )
    my_place = lax.axis_index(GROUP)
    mine = my_place + peers * lax.broadcasted_iota(jnp.int32, (1, halves, 1, 1), 1)
    member = jnp.any(routes_all[:, None] == mine, axis=3)
    order = (
        jnp.sum(
            (
                member[:, :, None, :]
                & (
                    lax.broadcasted_iota(jnp.int32, (row_count, row_count), 0)
                    >= lax.broadcasted_iota(jnp.int32, (row_count, row_count), 1)
                )
            ).astype(jnp.float32),
            axis=3,
        ).astype(jnp.int32)
        - 1
    )
    capacity = min(row_count, 9 * row_count * top_count // (8 * expert_count))
    capacity = -(-capacity // 32) * 32
    slot_of = jnp.where(member, order, -1)
    slot_ids = lax.broadcasted_iota(jnp.int32, (1, 1, capacity, 1), 2)
    select = (slot_of[:, :, None, :] == slot_ids).astype(jnp.bfloat16)

    cot_all = gather_rows(cot_low, GROUP).reshape(peers, row_count, model_width)

    w_out = gather_rows(to_low(out_weight), EVERY)
    w_shared_up = gather_rows(to_low(shared_gate_up), EVERY)
    w_shared_down = gather_rows(to_low(shared_down), EVERY)
    w_expert_up = gather_rows(to_low(expert_gate_up), HOLDERS)
    w_expert_up = w_expert_up.reshape(halves, model_width, w_expert_up.shape[2])
    w_expert_down = gather_rows(to_low(expert_down), HOLDERS)
    w_expert_down = w_expert_down.reshape(halves, -1, model_width)

    flat_in = dealt_in.reshape(row_count, model_width).astype(jnp.float32)
    normed, norm_one_back = jax.vjp(rms_scale, flat_in, gain_one.astype(jnp.float32))
    normed_low = normed.astype(jnp.bfloat16)
    projected = dot(normed_low, w_in)
    mixer_fn = partial(mixer_local, seq_count=seq_count, block_len=BLK)
    gated_out, mixer_back = jax.vjp(
        mixer_fn,
        projected,
        kernel_low.astype(jnp.float32),
        shift_low.astype(jnp.float32),
        step_bias,
        decay_log,
        skip_gain,
        gated_scale_low.astype(jnp.float32),
    )
    gated_low = gated_out.astype(jnp.bfloat16)
    middle = flat_in + dot(gated_low, w_out)
    normed_two, norm_two_back = jax.vjp(rms_scale, middle, gain_two.astype(jnp.float32))
    mid_low = normed_two.astype(jnp.bfloat16)

    rows_all = gather_rows(mid_low, GROUP).reshape(peers, row_count, model_width)
    logits = dot(mid_low, w_router)
    masked = jnp.where(chosen, logits, -jnp.inf)
    lifted = jnp.where(chosen, jnp.exp(masked - jnp.max(masked, axis=1, keepdims=True)), 0.0)
    gates = lifted / jnp.sum(lifted, axis=1, keepdims=True)
    gates_all = gather_rows(gates, GROUP).reshape(peers, row_count, expert_count)
    gates_mine = jnp.sum(
        jnp.where(
            lax.broadcasted_iota(jnp.int32, (1, halves, 1, expert_count), 3) == mine,
            gates_all[:, None],
            0.0,
        ),
        axis=3,
    )
    slot_gate = jnp.sum(jnp.where(slot_of[:, :, None, :] == slot_ids, gates_mine[:, :, None, :], 0.0), axis=3)

    def pick(rows):
        return jnp.einsum(
            "sect,std->escd", select, rows, preferred_element_type=jnp.float32
        ).astype(jnp.bfloat16)

    def place(slots):
        return (
            jnp.einsum("sect,escd->std", select, slots, preferred_element_type=jnp.float32)
            .astype(jnp.bfloat16)
            .reshape(peers * row_count, model_width)
        )

    slot_gate = jnp.moveaxis(slot_gate, 1, 0)[..., None]
    expert_in = pick(rows_all)
    expert_pre = jnp.einsum(
        "escd,edf->escf", expert_in, w_expert_up, preferred_element_type=jnp.float32
    )
    expert_full, expert_back = jax.vjp(swiglu, expert_pre)
    expert_act = expert_full.astype(jnp.bfloat16)
    expert_res = jnp.einsum(
        "escf,efd->escd", expert_act, w_expert_down, preferred_element_type=jnp.float32
    ).astype(jnp.bfloat16)
    expert_cot = pick(cot_all).astype(jnp.float32)
    slot_cot = (slot_gate * expert_cot).astype(jnp.bfloat16)
    slot_gate_cot = jnp.sum(expert_cot * expert_res.astype(jnp.float32), axis=3)
    gate_cot_rows = jnp.sum(
        jnp.where(
            slot_of[:, :, None, :] == slot_ids, jnp.moveaxis(slot_gate_cot, 0, 1)[..., None], 0.0
        ),
        axis=2,
    )
    act_cot = jnp.einsum(
        "escd,efd->escf", slot_cot, w_expert_down, preferred_element_type=jnp.float32
    )
    pre_cot = expert_back(act_cot)[0].astype(jnp.bfloat16)
    input_cot = jnp.einsum(
        "escf,edf->escd", pre_cot, w_expert_up, preferred_element_type=jnp.float32
    ).astype(jnp.bfloat16)
    rows_back = scatter_rows(place(input_cot), GROUP)
    gate_cot_back = lax.all_to_all(gate_cot_rows, GROUP, split_axis=0, concat_axis=0, tiled=True)
    gate_cot = jnp.moveaxis(gate_cot_back, 2, 0)
    gate_cot = jnp.moveaxis(gate_cot, 2, 1).reshape(row_count, expert_count)
    moe_out = scatter_rows(
        place((slot_gate * expert_res.astype(jnp.float32)).astype(jnp.bfloat16)), GROUP
    ).astype(jnp.float32)
    grad_down_local = jnp.einsum(
        "escf,escd->efd", expert_act, slot_cot, preferred_element_type=jnp.float32
    ).astype(jnp.bfloat16)
    grad_up_local = jnp.einsum(
        "escd,escf->edf", expert_in, pre_cot, preferred_element_type=jnp.float32
    ).astype(jnp.bfloat16)
    grad_expert_up = scatter_rows(
        grad_up_local.reshape((-1,) + expert_gate_up.shape[1:]), HOLDERS
    ).astype(jnp.float32)
    grad_expert_down = scatter_rows(
        grad_down_local.reshape((-1,) + expert_down.shape[1:]), HOLDERS
    ).astype(jnp.float32)

    shared_pre = dot(mid_low, w_shared_up)
    shared_full, shared_back = jax.vjp(swiglu, shared_pre)
    shared_act = shared_full.astype(jnp.bfloat16)
    shared_out = dot(shared_act, w_shared_down)
    grad_shared_down = dot_left(shared_act, cot_low).astype(jnp.bfloat16)
    shared_pre_cot = shared_back(dot_right(cot_low, w_shared_down))[0].astype(jnp.bfloat16)
    grad_shared_up = dot_left(mid_low, shared_pre_cot).astype(jnp.bfloat16)
    shared_in_cot = dot_right(shared_pre_cot, w_shared_up)
    sum_shared_down = scatter_rows(grad_shared_down, EVERY).astype(jnp.float32)
    sum_shared_up = scatter_rows(grad_shared_up, EVERY).astype(jnp.float32)

    logit_cot = (gates * (gate_cot - jnp.sum(gates * gate_cot, axis=1, keepdims=True))).astype(
        jnp.bfloat16
    )
    grad_router = dot_left(mid_low, logit_cot)
    mid_cot = rows_back.astype(jnp.float32) + dot_right(logit_cot, w_router) + shared_in_cot
    middle_norm_cot, gain_two_cot = norm_two_back(mid_cot)
    middle_cot = row_cot + middle_norm_cot
    branch_cot = middle_cot.astype(jnp.bfloat16)
    block_out = (
        (valid_rows * (middle + moe_out + shared_out))
        .astype(jnp.bfloat16)
        .reshape(seq_count, length, model_width)
    )
    back_out = lax.all_to_all(block_out, "dp", split_axis=1, concat_axis=0, tiled=True)
    grad_out = dot_left(gated_low, branch_cot).astype(jnp.bfloat16)
    sum_out = scatter_rows(grad_out, EVERY).astype(jnp.float32)
    proj_cot, kernel_cot, shift_cot, step_cot, decay_cot, skip_cot, gated_gain_cot = mixer_back(
        dot_right(branch_cot, w_out)
    )
    proj_low = proj_cot.astype(jnp.bfloat16)
    grad_in = dot_left(normed_low, proj_low).astype(jnp.bfloat16)
    sum_in = scatter_rows(grad_in, EVERY).astype(jnp.float32)
    flat_norm_cot, gain_one_cot = norm_one_back(dot_right(proj_low, w_in))
    input_grad = (
        (middle_cot + flat_norm_cot).astype(jnp.bfloat16).reshape(seq_count, length, model_width)
    )
    back_grad = lax.all_to_all(input_grad, "dp", split_axis=1, concat_axis=0, tiled=True)

    heads = jnp.concatenate([step_cot, decay_cot, skip_cot])
    small_cots = [gain_one_cot, kernel_cot, shift_cot, gated_gain_cot, gain_two_cot, grad_router]
    shares = [v.reshape(device_total, -1) for v in small_cots]
    shares.append(jnp.broadcast_to(heads[None], (device_total, heads.shape[0])))
    small_sum = scatter_rows(jnp.concatenate(shares, axis=1), EVERY)[0]
    sums = []
    offset = 0
    for v in small:
        sums.append(small_sum[offset : offset + v.size].reshape(v.shape))
        offset += v.size
    head_count = step_bias.shape[0]
    head_sums = small_sum[offset:].reshape(3, head_count)
    final_out = jnp.take(back_out, seq_order, axis=0)
    final_grad = jnp.take(back_grad, seq_order, axis=0)
    return (
        final_out,
        final_grad,
        sums[0],
        sum_in,
        sums[1],
        sums[2],
        head_sums[0],
        head_sums[1],
        head_sums[2],
        sums[3],
        sum_out,
        sums[4],
        sums[5],
        grad_expert_up,
        grad_expert_down,
        sum_shared_up,
        sum_shared_down,
    )


def solution(mesh):
    fine = Mesh(
        mesh.devices.reshape((mesh.shape["dp"], 2, 2, 2, mesh.shape["expert"] // 8)), EVERY
    )
    rows = P(SPLIT, "dp", None)
    flat = P(EVERY)
    split = P(EVERY, None)
    in_specs = (
        rows,
        rows,
        P(SPLIT),
        P(SPLIT),
        P(EVERY, None, None),
        flat,
        split,
        split,
        flat,
        P(),
        P(),
        P(),
        flat,
        split,
        flat,
        split,
        rows,
        rows,
        split,
        split,
    )
    out_specs = (
        rows,
        rows,
        flat,
        split,
        split,
        flat,
        P(),
        P(),
        P(),
        flat,
        split,
        flat,
        split,
        rows,
        rows,
        split,
        split,
    )
    return jax.shard_map(local, mesh=fine, in_specs=in_specs, out_specs=out_specs, check_vma=False)
```

```python
from functools import partial

import jax
import jax.numpy as jnp
from jax import lax
from jax.experimental import pallas as pl
from jax.experimental.pallas import tpu as pltpu
from jax.sharding import Mesh, PartitionSpec as P

BLK = 128
LANES = 128
INTERPRET = False
NEVER = -1e30
EPSILON = 1e-05
FULL_PRECISION = lax.Precision.HIGHEST
SPLIT = ("e3", "e2", "e1", "e0")
EVERY = ("dp",) + SPLIT
GROUP = SPLIT[1:]


def rms_scale(values, gain_row):
    return (
        values * lax.rsqrt(jnp.mean(values * values, axis=-1, keepdims=True) + EPSILON) * gain_row
    )


def swiglu(pre_act):
    half_width = pre_act.shape[-1] // 2
    return jax.nn.silu(pre_act[..., :half_width]) * pre_act[..., half_width:]


def mm(left_mat, right_mat, left_dim=1, right_dim=0):
    return lax.dot_general(
        left_mat,
        right_mat,
        (((left_dim,), (right_dim,)), ((), ())),
        preferred_element_type=jnp.float32,
    )


def mm_parts(values, ones, right_dim=0):
    high = values.astype(jnp.bfloat16)
    rest = values - high.astype(jnp.float32)
    mid = rest.astype(jnp.bfloat16)
    low = (rest - mid.astype(jnp.float32)).astype(jnp.bfloat16)
    return (
        mm(high, ones, 1, right_dim) + mm(mid, ones, 1, right_dim) + mm(low, ones, 1, right_dim)
    )


def mm_full(left_mat, right_mat):
    return lax.dot_general(
        left_mat,
        right_mat,
        (((1,), (0,)), ((), ())),
        precision=FULL_PRECISION,
        preferred_element_type=jnp.float32,
    )


def iotas(size):
    return (
        lax.broadcasted_iota(jnp.int32, (size, LANES), 0),
        lax.broadcasted_iota(jnp.int32, (size, LANES), 1),
    )


def step_terms(raw, bias, decay, spread, ran, steps, run_rows):
    size = raw.shape[0]
    down, across = iotas(size)
    shifted = raw + bias
    step = jnp.maximum(shifted, 0.0) + jnp.log1p(jnp.exp(-jnp.abs(shifted)))
    rate = -jnp.exp(decay) * step
    run = mm_full((down >= across).astype(jnp.float32), rate)
    ran[...] = mm_parts(run, spread)
    steps[...] = mm_parts(step, spread)
    run_rows[...] = run.T
    return shifted, step, rate


def conv_at(ext, taps, shift, cols, size, width):
    total = shift[:, cols]
    for tap in range(width):
        total = total + taps[tap : tap + 1, cols] * ext[pl.ds(9 - width + tap, size), cols]
    return total


def scan_kernel(
    mixed, taps, shift, bias, decay, skip, spread, y_out, before_out,
    ext, state, ran, steps, run_rows, crossed, fed,
    *, width,
):
    size = mixed.shape[0]
    inner = skip.shape[1]
    channels = shift.shape[1]
    wide = inner // LANES
    head = channels

    @pl.when(pl.program_id(0) == 0)
    def _():
        ext[pl.ds(0, 8), :] = jnp.zeros((8, channels), jnp.float32)
        state[...] = jnp.zeros_like(state)

    @pl.when(pl.program_id(0) > 0)
    def _():
        ext[pl.ds(0, 8), :] = ext[pl.ds(size, 8), :]

    ext[pl.ds(8, size), :] = mixed[:, :channels]
    step_terms(mixed[:, head:], bias[...], decay[...], spread[...], ran, steps, run_rows)
    down, across = iotas(size)
    causal = down >= across
    first = across < LANES // 2
    keep = jax.nn.silu(conv_at(ext, taps, shift, pl.ds(inner, LANES), size, width))
    read = jax.nn.silu(conv_at(ext, taps, shift, pl.ds(inner + LANES, LANES), size, width))
    read_low = read.astype(jnp.bfloat16)
    scores = mm(read_low, keep.astype(jnp.bfloat16), 1, 1)
    crossed[...] = mm(read_low, state[...].astype(jnp.bfloat16))
    before_out[0] = state[...]

    def pair(number, carry):
        cols = pl.ds(pl.multiple_of(number * LANES, LANES), LANES)
        x = jax.nn.silu(conv_at(ext, taps, shift, cols, size, width))
        run = ran[:, cols]
        stepped = x * steps[:, cols]
        stepped_low = stepped.astype(jnp.bfloat16)
        inside = []
        for one in range(2):
            at_row = jnp.broadcast_to(run[:, one * (LANES // 2)][:, None], (size, LANES))
            at_col = run_rows[pl.ds(2 * number + one, 1), :]
            mix = scores * jnp.exp(jnp.where(causal, at_row - at_col, NEVER))
            inside.append(mm(mix.astype(jnp.bfloat16), stepped_low))
        y_out[:, cols] = (
            jnp.where(first, inside[0], inside[1])
            + jnp.exp(run) * crossed[:, cols]
            + skip[:, cols] * x
        )
        fed[:, cols] = (stepped * jnp.exp(run[size - 1 :, :] - run)).astype(jnp.bfloat16)
        return carry

    lax.fori_loop(0, wide, pair, 0)
    state[...] = jnp.exp(ran[pl.ds(size - 1, 1), :]) * state[...] + mm(
        keep.T.astype(jnp.bfloat16), fed[...]
    )


def scan_back_kernel(
    mixed, halo, y_cot, before, taps, shift, bias, decay, skip, spread,
    mixed_cot, taps_cot, shift_cot, skip_cot, bias_cot, decay_cot,
    ext, cot_ext, after, ran, steps, run_rows, crossed, kept, spill, turned, fed, heard, col_rows, scores_cot, ends,
    *, width,
):
    size = mixed.shape[0]
    inner = skip.shape[1]
    channels = shift.shape[1]
    wide = inner // LANES
    head = channels
    half = LANES // 2
    started = pl.program_id(0) == 0

    @pl.when(started)
    def _():
        cot_ext[pl.ds(size, 8), :] = jnp.zeros((8, channels), jnp.float32)
        after[...] = jnp.zeros_like(after)
        taps_cot[...] = jnp.zeros_like(taps_cot)
        shift_cot[...] = jnp.zeros_like(shift_cot)
        skip_cot[...] = jnp.zeros_like(skip_cot)
        bias_cot[...] = jnp.zeros_like(bias_cot)
        decay_cot[...] = jnp.zeros_like(decay_cot)

    @pl.when(jnp.logical_not(started))
    def _():
        cot_ext[pl.ds(size, 8), :] = cot_ext[pl.ds(0, 8), :]

    top = pl.program_id(0) == pl.num_programs(0) - 1
    ext[pl.ds(0, 8), :] = jnp.where(top, 0.0, halo[:, :channels])
    ext[pl.ds(8, size), :] = mixed[:, :channels]
    shifted, step, rate = step_terms(
        mixed[:, head:], bias[...], decay[...], spread[...], ran, steps, run_rows
    )
    down, across = iotas(size)
    later = across >= down
    first = across < half
    keep_cols = pl.ds(inner, LANES)
    read_cols = pl.ds(inner + LANES, LANES)
    keep_pre = conv_at(ext, taps, shift, keep_cols, size, width)
    read_pre = conv_at(ext, taps, shift, read_cols, size, width)
    keep, read = jax.nn.silu(keep_pre), jax.nn.silu(read_pre)
    keep_low, read_low = keep.astype(jnp.bfloat16), read.astype(jnp.bfloat16)
    scores = mm(keep_low, read_low, 1, 1)
    before_low = before[0].astype(jnp.bfloat16)
    after_low = after[...].astype(jnp.bfloat16)
    crossed[...] = mm(read_low, before_low)
    kept[...] = mm(keep_low, after_low)
    scores_cot[...] = jnp.zeros_like(scores_cot)
    col_rows[...] = jnp.zeros_like(col_rows)

    def finish(cols, pre, cot):
        gate = jax.nn.sigmoid(pre)
        cot = cot * (gate * (1.0 + pre * (1.0 - gate)))
        cot_ext[pl.ds(0, size), cols] = cot
        total = None
        for tap in range(width):
            part = taps[tap : tap + 1, cols] * cot_ext[pl.ds(width - 1 - tap, size), cols]
            total = part if total is None else total + part
            taps_cot[tap : tap + 1, cols] += jnp.sum(
                cot * ext[pl.ds(9 - width + tap, size), cols], axis=0, keepdims=True
            )
        shift_cot[:, cols] += jnp.sum(cot, axis=0, keepdims=True)
        mixed_cot[:, cols] = total.astype(jnp.bfloat16)

    def pair(number, carry):
        cols = pl.ds(pl.multiple_of(number * LANES, LANES), LANES)
        pre = conv_at(ext, taps, shift, cols, size, width)
        x = jax.nn.silu(pre)
        run = ran[:, cols]
        last = run[size - 1 :, :]
        steps_here = steps[:, cols]
        stepped = x * steps_here
        fade = jnp.exp(last - run)
        reach = jnp.exp(run)
        cot = y_cot[:, cols]
        cot_low = cot.astype(jnp.bfloat16)
        from_state = kept[:, cols] * fade
        sums, inside = [], []
        for one in range(2):
            at_row = jnp.broadcast_to(run[:, one * half][:, None], (size, LANES))
            at_col = run_rows[pl.ds(2 * number + one, 1), :]
            decayed = jnp.exp(jnp.where(later, at_col - at_row, NEVER))
            mine = first if one == 0 else jnp.logical_not(first)
            mix_cot = mm(jnp.where(mine, stepped, 0.0).astype(jnp.bfloat16), cot_low, 1, 1)
            decayed_cot = mix_cot * decayed
            scores_cot[...] += decayed_cot
            moved = decayed_cot * scores
            sums.append(jnp.sum(moved, axis=1, keepdims=True))
            col_rows[pl.ds(2 * number + one, 1), :] = jnp.sum(moved, axis=0, keepdims=True)
            inside.append(mm((scores * decayed).astype(jnp.bfloat16), cot_low))
        stepped_cot = jnp.where(first, inside[0], inside[1]) + from_state
        heard_here = reach * cot
        passed = stepped * from_state
        spill[:, cols] = (
            heard_here * crossed[:, cols]
            - passed
            - jnp.where(first, sums[0], sums[1]) * (1.0 / half)
        )
        turned[:, cols] = x * stepped_cot
        ends[:, cols] = jnp.sum(passed, axis=0, keepdims=True) + jnp.exp(last) * jnp.sum(
            before[0, :, cols] * after[:, cols], axis=0, keepdims=True
        )
        skip_cot[:, cols] += jnp.sum(x * cot, axis=0, keepdims=True)
        heard[:, cols] = heard_here.astype(jnp.bfloat16)
        fed[:, cols] = (stepped * fade).astype(jnp.bfloat16)
        finish(cols, pre, steps_here * stepped_cot + skip[:, cols] * cot)
        return carry

    lax.fori_loop(0, wide, pair, 0)
    scores_cot_low = scores_cot[...].astype(jnp.bfloat16)
    scores_cot_turned = scores_cot[...].T.astype(jnp.bfloat16)
    read_cot = mm(heard[...], before_low, 1, 1) + mm(scores_cot_turned, keep_low)
    keep_cot = mm(fed[...], after_low, 1, 1) + mm(scores_cot_low, read_low)
    finish(keep_cols, keep_pre, keep_cot)
    finish(read_cols, read_pre, read_cot)
    run_cot = mm_parts(spill[...], spread[...], 1) + col_rows[...].T
    end_cot = mm_parts(jnp.broadcast_to(ends[...], (8, inner)), spread[...], 1)[0:1]
    run_cot = run_cot + jnp.where(down == size - 1, end_cot, 0.0)
    rate_cot = mm_full(later.astype(jnp.float32), run_cot)
    step_cot = mm_parts(turned[...], spread[...], 1) - jnp.exp(decay[...]) * rate_cot
    raw_cot = step_cot * jax.nn.sigmoid(shifted)
    bias_cot[...] += jnp.sum(raw_cot, axis=0, keepdims=True)
    decay_cot[...] += jnp.sum(rate_cot * rate, axis=0, keepdims=True)
    mixed_cot[:, head:] = raw_cot.astype(jnp.bfloat16)
    after[...] = jnp.exp(ran[pl.ds(size - 1, 1), :]) * after[...] + mm(
        read.T.astype(jnp.bfloat16), heard[...]
    )


def whole(shape):
    return pl.BlockSpec(shape, lambda step: (0,) * len(shape))


def head_spread(heads, inner):
    return (
        lax.broadcasted_iota(jnp.int32, (LANES, inner), 0)
        == lax.broadcasted_iota(jnp.int32, (LANES, inner), 1) // (inner // heads)
    ).astype(jnp.bfloat16)


def scan_forward(mixed, taps, shift, bias, decay, skip, spread, block_len):
    rows, total = mixed.shape
    inner = skip.shape[1]
    channels = shift.shape[1]
    blocks = rows // block_len
    state_width = (channels - inner) // 2
    f32, low = jnp.float32, jnp.bfloat16
    return pl.pallas_call(
        partial(scan_kernel, width=taps.shape[0]),
        grid=(blocks,),
        in_specs=[
            pl.BlockSpec((block_len, total), lambda step: (step, 0)),
            whole(taps.shape),
            whole(shift.shape),
            whole(bias.shape),
            whole(decay.shape),
            whole(skip.shape),
            whole(spread.shape),
        ],
        out_specs=[
            pl.BlockSpec((block_len, inner), lambda step: (step, 0)),
            pl.BlockSpec((1, state_width, inner), lambda step: (step, 0, 0)),
        ],
        out_shape=[
            jax.ShapeDtypeStruct((rows, inner), f32),
            jax.ShapeDtypeStruct((blocks, state_width, inner), f32),
        ],
        scratch_shapes=[
            pltpu.VMEM((block_len + 8, channels), f32),
            pltpu.VMEM((state_width, inner), f32),
            pltpu.VMEM((block_len, inner), f32),
            pltpu.VMEM((block_len, inner), f32),
            pltpu.VMEM((LANES, block_len), f32),
            pltpu.VMEM((block_len, inner), f32),
            pltpu.VMEM((block_len, inner), low),
        ],
        compiler_params=pltpu.CompilerParams(vmem_limit_bytes=48 << 20),
        cost_estimate=pl.CostEstimate(
            flops=10**9, transcendentals=10**7, bytes_accessed=120 * 10**6
        ),
        interpret=INTERPRET,
        name="scan_forward",
    )(mixed, taps, shift, bias, decay, skip, spread)


def scan_backward(mixed, y_cot, before, taps, shift, bias, decay, skip, spread, block_len):
    rows, total = mixed.shape
    inner = skip.shape[1]
    channels = shift.shape[1]
    blocks = rows // block_len
    state_width = (channels - inner) // 2
    f32, low = jnp.float32, jnp.bfloat16
    eighths = block_len // 8
    back = blocks - 1
    return pl.pallas_call(
        partial(scan_back_kernel, width=taps.shape[0]),
        grid=(blocks,),
        in_specs=[
            pl.BlockSpec((block_len, total), lambda step: (back - step, 0)),
            pl.BlockSpec(
                (8, total), lambda step: (jnp.maximum((back - step) * eighths - 1, 0), 0)
            ),
            pl.BlockSpec((block_len, inner), lambda step: (back - step, 0)),
            pl.BlockSpec((1, state_width, inner), lambda step: (back - step, 0, 0)),
            whole(taps.shape),
            whole(shift.shape),
            whole(bias.shape),
            whole(decay.shape),
            whole(skip.shape),
            whole(spread.shape),
        ],
        out_specs=[
            pl.BlockSpec((block_len, total), lambda step: (back - step, 0)),
            whole(taps.shape),
            whole(shift.shape),
            whole(skip.shape),
            whole(bias.shape),
            whole(decay.shape),
        ],
        out_shape=[
            jax.ShapeDtypeStruct((rows, total), low),
            jax.ShapeDtypeStruct(taps.shape, f32),
            jax.ShapeDtypeStruct(shift.shape, f32),
            jax.ShapeDtypeStruct(skip.shape, f32),
            jax.ShapeDtypeStruct(bias.shape, f32),
            jax.ShapeDtypeStruct(decay.shape, f32),
        ],
        scratch_shapes=[
            pltpu.VMEM((block_len + 8, channels), f32),
            pltpu.VMEM((block_len + 8, channels), f32),
            pltpu.VMEM((state_width, inner), f32),
            pltpu.VMEM((block_len, inner), f32),
            pltpu.VMEM((block_len, inner), f32),
            pltpu.VMEM((LANES, block_len), f32),
            pltpu.VMEM((block_len, inner), f32),
            pltpu.VMEM((block_len, inner), f32),
            pltpu.VMEM((block_len, inner), f32),
            pltpu.VMEM((block_len, inner), f32),
            pltpu.VMEM((block_len, inner), low),
            pltpu.VMEM((block_len, inner), low),
            pltpu.VMEM((LANES, block_len), f32),
            pltpu.VMEM((block_len, block_len), f32),
            pltpu.VMEM((1, inner), f32),
        ],
        compiler_params=pltpu.CompilerParams(vmem_limit_bytes=56 << 20),
        cost_estimate=pl.CostEstimate(
            flops=2 * 10**9, transcendentals=10**7, bytes_accessed=240 * 10**6
        ),
        interpret=INTERPRET,
        name="scan_backward",
    )(mixed, mixed, y_cot, before, taps, shift, bias, decay, skip, spread)


def dot_right(left_mat, right_mat):
    return lax.dot_general(
        left_mat, right_mat, (((1,), (1,)), ((), ())), preferred_element_type=jnp.float32
    )


def dot_left(left_mat, right_mat):
    return lax.dot_general(
        left_mat, right_mat, (((0,), (0,)), ((), ())), preferred_element_type=jnp.float32
    )


def to_low(weight):
    return weight.astype(jnp.bfloat16)


def gather_rows(block, axes):
    return lax.all_gather(block, axes, axis=0, tiled=True)


def tell(row, axes):
    return lax.all_to_all(
        jnp.broadcast_to(row, (lax.axis_size(axes),) + row.shape[1:]),
        axes,
        split_axis=0,
        concat_axis=0,
        tiled=True,
    )


def scatter_rows(block, axes):
    return lax.psum_scatter(block, axes, scatter_dimension=0, tiled=True)


def dot(left_mat, right_mat):
    return jnp.dot(left_mat, right_mat, preferred_element_type=jnp.float32)


def swap(block, axis):
    return lax.ppermute(block, axis, [(0, 1), (1, 0)])


def after(value, *others):
    return lax.optimization_barrier((value,) + others)[0]


def spread_rows(block, second, third, gates):
    if lax.axis_size(second) != 2:
        second, third = third, second
    whole_block = block.reshape((1,) * len(EVERY) + block.shape)
    for axis, gate in zip(("e3", "e2", third, second, "e0"), gates):
        at = EVERY.index(axis)
        if lax.axis_size(axis) == 2:
            came = swap(whole_block, axis)
            if gate is not None:
                came = after(came, gate)
            whole_block = join(whole_block, came, lax.axis_index(axis), at)
        else:
            whole_block = lax.all_gather(whole_block, axis, axis=at, tiled=True)
    return whole_block.reshape(-1, block.shape[1])


def take(block, place, axis_at):
    return lax.dynamic_index_in_dim(block, place, axis_at, keepdims=False)


def fold(block, layout, order):
    layout = list(layout)
    for axis in order:
        at = layout.index(axis)
        if lax.axis_size(axis) == 2:
            place = lax.axis_index(axis)
            came = swap(take(block, 1 - place, at), axis)
            block = add(take(block, place, at), came)
        else:
            block = lax.psum_scatter(block, axis, scatter_dimension=at, tiled=False)
        layout.pop(at)
    return block


def add(one, other):
    return (one.astype(jnp.float32) + other.astype(jnp.float32)).astype(one.dtype)


class WeightGrad:
    def __init__(self, left_mat, right_mat, second, third):
        sizes = [lax.axis_size(axis) for axis in EVERY]
        if lax.axis_size(second) != 2:
            second, third = third, second
        self.second = second
        self.order = [third, "e2", "e3"]
        self.inner = left_mat.shape[0]
        self.left_rows = left_mat.T.reshape(sizes + [-1, self.inner])
        self.right_mat = right_mat
        self.layout = [axis for axis in EVERY if axis not in ("e0", second)]
        self.one, self.two = lax.axis_index("e0"), lax.axis_index(second)
        self.far = swap(self.piece(1 - self.one, 1 - self.two).astype(jnp.bfloat16), "e0")
        self.near = swap(self.piece(1 - self.one, self.two).astype(jnp.bfloat16), "e0")

    def piece(self, place_one, place_two):
        part = take(self.left_rows, place_one, EVERY.index("e0"))
        part = take(part, place_two, EVERY.index(self.second))
        return dot(part.reshape(-1, self.inner), self.right_mat)

    def send(self):
        far = self.piece(self.one, 1 - self.two) + self.far.astype(jnp.float32)
        self.sent = far.astype(jnp.bfloat16)
        near = self.piece(self.one, self.two) + self.near.astype(jnp.float32)
        self.kept = near.astype(jnp.bfloat16)
        self.axis = self.second
        return self

    def start(self, *gates):
        self.before = self.kept if self.sent is None else self.sent
        if self.sent is not None:
            self.sent = swap(after(self.sent, *gates) if gates else self.sent, self.axis)
        return self

    def step(self, *gates):
        block = self.kept
        if self.sent is not None:
            block = add(block, after(self.sent, *gates) if gates else self.sent)
        if self.axis == self.second:
            share = self.left_rows.shape[5]
            block = block.reshape([lax.axis_size(axis) for axis in self.layout] + [share, -1])
        if not self.order:
            self.total = block.astype(jnp.float32)
            return self
        self.axis = self.order.pop(0)
        at = self.layout.index(self.axis)
        self.layout.pop(at)
        if lax.axis_size(self.axis) == 2:
            place = lax.axis_index(self.axis)
            self.kept, self.sent = take(block, place, at), take(block, 1 - place, at)
        else:
            self.kept = lax.psum_scatter(block, self.axis, scatter_dimension=at, tiled=False)
            self.sent = None
        return self

    def finish(self):
        while self.order:
            self.step().start()
        return self.step().total


def join(mine, other, place, axis_at):
    return jnp.where(
        place == 0,
        jnp.concatenate([mine, other], axis=axis_at),
        jnp.concatenate([other, mine], axis=axis_at),
    )


def gather_halves(both, gate):
    if lax.axis_size("dp") == 2:
        return join(both, after(swap(both, "dp"), gate), lax.axis_index("dp"), 1)
    return lax.all_gather(both, "dp", axis=1, tiled=True)


def local(
    tokens_in,
    out_grad,
    seq_lengths,
    seq_order,
    routes_top,
    norm_gain,
    in_weight,
    conv_weight,
    conv_bias,
    step_bias,
    decay_log,
    skip_gain,
    gated_gain,
    out_weight,
    ffn_gain,
    router_weight,
    expert_gate_up,
    expert_down,
    shared_gate_up,
    shared_down,
):
    group_count = lax.axis_size("dp")
    my_rank = lax.axis_index("dp")
    peers = lax.axis_size(GROUP)
    halves = lax.axis_size("e3")
    device_total = lax.axis_size(EVERY)

    small = [norm_gain, conv_weight, conv_bias, gated_gain, ffn_gain, router_weight]
    small_flat = jnp.concatenate([to_low(v).reshape(1, -1) for v in small], axis=1)
    small_all = tell(small_flat, EVERY)
    smalls = []
    offset = 0
    for v in small:
        smalls.append(
            small_all[:, offset : offset + v.size].reshape((device_total * v.shape[0],) + v.shape[1:])
        )
        offset += v.size
    gain_one, kernel_low, shift_low, gated_scale_low, gain_two, w_router = smalls

    slot_rows = lax.broadcasted_iota(jnp.int32, (group_count, group_count), 0)
    slot_cols = lax.broadcasted_iota(jnp.int32, (group_count, group_count), 1)
    picks = (seq_order[None, :] == slot_rows).astype(jnp.int32)
    inverse = jnp.sum(picks * slot_cols, axis=1)
    my_length = jnp.sum(jnp.where(seq_order == my_rank, seq_lengths, 0))
    dealt_in, dealt_grad = (
        lax.all_to_all(
            jnp.take(block, inverse, axis=0), "dp", split_axis=0, concat_axis=0, tiled=True
        )
        for block in (tokens_in, out_grad)
    )
    model_width = tokens_in.shape[2]
    row_count = dealt_in.shape[0] * dealt_in.shape[1]
    top_count = routes_top.shape[2]
    expert_count = w_router.shape[1]
    positions = lax.broadcasted_iota(jnp.int32, (row_count, 1), 0)
    valid = positions < my_length
    valid_rows = valid.astype(jnp.float32)
    cot_low = jnp.where(valid, dealt_grad.reshape(row_count, model_width), 0)
    row_cot = cot_low.astype(jnp.float32)

    gate_width = gated_gain.shape[0] * device_total
    head_count = step_bias.shape[0]
    pad_heads = ((0, 0), (0, LANES - head_count))
    w_scan = gather_rows(jnp.pad(to_low(in_weight[:, gate_width:]), pad_heads), EVERY)
    w_gate = gather_rows(to_low(in_weight[:, :gate_width]), EVERY)
    routes = routes_top.reshape(row_count, top_count)
    expert_ids = lax.broadcasted_iota(jnp.int32, (1, expert_count), 1)
    chosen = jnp.any(routes[:, :, None] == expert_ids[:, None, :], axis=1)
    routes_all = tell(jnp.where(valid, routes, -1)[None], GROUP)
    up_low, down_low, out_low = lax.optimization_barrier(
        (
            to_low(expert_gate_up),
            to_low(expert_down),
            to_low(out_weight),
            small_all,
            routes_all,
            dealt_in,
        )
    )[:3]
    my_place = lax.axis_index(GROUP)
    mine = my_place + peers * (
        lax.axis_index("e3") ^ lax.broadcasted_iota(jnp.int32, (1, halves, 1, 1), 1)
    )
    member = jnp.any(routes_all[:, None] == mine, axis=3)
    order = (
        jnp.sum(
            (
                member[:, :, None, :]
                & (
                    lax.broadcasted_iota(jnp.int32, (row_count, row_count), 0)
                    >= lax.broadcasted_iota(jnp.int32, (row_count, row_count), 1)
                )
            ).astype(jnp.float32),
            axis=3,
        ).astype(jnp.int32)
        - 1
    )
    capacity = min(row_count, 9 * row_count * top_count // (8 * expert_count))
    capacity = -(-capacity // 32) * 32
    slot_of = jnp.where(member, order, -1)
    slot_ids = lax.broadcasted_iota(jnp.int32, (1, 1, capacity, 1), 2)
    select = (slot_of[:, :, None, :] == slot_ids).astype(jnp.bfloat16)


    w_shared_up = gather_rows(to_low(shared_gate_up), EVERY)
    w_shared_down = gather_rows(to_low(shared_down), EVERY)

    flat_in = dealt_in.reshape(row_count, model_width).astype(jnp.float32)
    normed, norm_one_back = jax.vjp(rms_scale, flat_in, gain_one.astype(jnp.float32))
    normed_low = normed.astype(jnp.bfloat16)
    normed_low = after(normed_low, slot_of)
    mixed = dot(normed_low, w_scan)
    scan_args = (
        kernel_low.astype(jnp.float32).T,
        shift_low.astype(jnp.float32)[None],
        jnp.pad(step_bias[None], pad_heads),
        jnp.pad(decay_log[None], pad_heads),
        jnp.repeat(skip_gain, gate_width // head_count)[None],
        head_spread(head_count, gate_width),
    )
    scanned, before = scan_forward(mixed, *scan_args, BLK)
    up_both = jnp.concatenate([up_low, after(swap(up_low, "e3"), mixed)], axis=0)
    down_both = jnp.concatenate([down_low, after(swap(down_low, "e3"), mixed)], axis=0)
    gate_part = dot(normed_low, w_gate)
    gated_out, gated_back = jax.vjp(
        lambda scan, gate, gain: rms_scale(scan * jax.nn.silu(gate), gain),
        scanned,
        gate_part,
        gated_scale_low.astype(jnp.float32),
    )
    gated_low = gated_out.astype(jnp.bfloat16)
    w_out = spread_rows(out_low, "e1", "dp", (None, None, None, scanned, gated_low))
    middle = flat_in + dot(gated_low, w_out)
    normed_two, norm_two_back = jax.vjp(rms_scale, middle, gain_two.astype(jnp.float32))
    mid_low = normed_two.astype(jnp.bfloat16)

    w_expert_up = gather_halves(up_both, mid_low)
    w_expert_down = gather_halves(down_both, mid_low)

    rows_all = gather_rows(mid_low, GROUP).reshape(peers, row_count, model_width)
    cot_all = gather_rows(after(cot_low, rows_all), GROUP).reshape(peers, row_count, model_width)
    logits = dot(mid_low, w_router)
    masked = jnp.where(chosen, logits, -jnp.inf)
    lifted = jnp.where(chosen, jnp.exp(masked - jnp.max(masked, axis=1, keepdims=True)), 0.0)
    gates = lifted / jnp.sum(lifted, axis=1, keepdims=True)
    by_peer = gates.T.reshape(halves, peers, row_count)
    by_peer = jnp.where(lax.axis_index("e3") == 0, by_peer, by_peer[::-1])
    gates_mine = lax.all_to_all(
        jnp.moveaxis(by_peer, 1, 0), GROUP, split_axis=0, concat_axis=0, tiled=True
    )
    slot_gate = jnp.sum(jnp.where(slot_of[:, :, None, :] == slot_ids, gates_mine[:, :, None, :], 0.0), axis=3)

    def pick(rows):
        return jnp.einsum(
            "sect,std->escd", select, rows, preferred_element_type=jnp.float32
        ).astype(jnp.bfloat16)

    def place(slots):
        return (
            jnp.einsum("sect,escd->std", select, slots, preferred_element_type=jnp.float32)
            .astype(jnp.bfloat16)
            .reshape(peers * row_count, model_width)
        )

    slot_gate = jnp.moveaxis(slot_gate, 1, 0)[..., None]
    expert_in = pick(rows_all)
    expert_pre = jnp.einsum(
        "escd,edf->escf", expert_in, w_expert_up, preferred_element_type=jnp.float32
    )
    expert_full, expert_back = jax.vjp(swiglu, expert_pre)
    expert_act = expert_full.astype(jnp.bfloat16)
    expert_res = jnp.einsum(
        "escf,efd->escd", expert_act, w_expert_down, preferred_element_type=jnp.float32
    ).astype(jnp.bfloat16)
    expert_cot = pick(cot_all).astype(jnp.float32)
    slot_cot = (slot_gate * expert_cot).astype(jnp.bfloat16)
    slot_gate_cot = jnp.sum(expert_cot * expert_res.astype(jnp.float32), axis=3)
    gate_cot_rows = jnp.sum(
        jnp.where(
            slot_of[:, :, None, :] == slot_ids, jnp.moveaxis(slot_gate_cot, 0, 1)[..., None], 0.0
        ),
        axis=2,
    )
    act_cot = jnp.einsum(
        "escd,efd->escf", slot_cot, w_expert_down, preferred_element_type=jnp.float32
    )
    pre_cot = expert_back(act_cot)[0].astype(jnp.bfloat16)
    input_cot = jnp.einsum(
        "escf,edf->escd", pre_cot, w_expert_up, preferred_element_type=jnp.float32
    ).astype(jnp.bfloat16)
    rows_back = scatter_rows(place(input_cot), GROUP)
    gate_cot_back = lax.all_to_all(gate_cot_rows, GROUP, split_axis=0, concat_axis=0, tiled=True)
    gate_cot = jnp.moveaxis(gate_cot_back, 2, 0)
    gate_cot = jnp.where(lax.axis_index("e3") == 0, gate_cot, gate_cot[:, :, ::-1])
    gate_cot = jnp.moveaxis(gate_cot, 2, 1).reshape(row_count, expert_count)
    moe_slots = (slot_gate * expert_res.astype(jnp.float32)).astype(jnp.bfloat16)
    moe_out = scatter_rows(after(place(moe_slots), rows_back), GROUP).astype(jnp.float32)
    grad_down_local = jnp.einsum(
        "escf,escd->efd", expert_act, slot_cot, preferred_element_type=jnp.float32
    ).astype(jnp.bfloat16)
    grad_up_local = jnp.einsum(
        "escd,escf->edf", expert_in, pre_cot, preferred_element_type=jnp.float32
    ).astype(jnp.bfloat16)
    shared_pre = dot(mid_low, w_shared_up)
    shared_full, shared_back = jax.vjp(swiglu, shared_pre)
    shared_act = shared_full.astype(jnp.bfloat16)
    shared_out = dot(shared_act, w_shared_down)
    shared_pre_cot = shared_back(dot_right(cot_low, w_shared_down))[0].astype(jnp.bfloat16)
    shared_in_cot = dot_right(shared_pre_cot, w_shared_up)

    share_down = WeightGrad(shared_act, cot_low, "dp", "e1")
    share_up = WeightGrad(mid_low, shared_pre_cot, "e1", "dp")
    expert_parts = []
    for block in (grad_up_local, grad_down_local):
        block = block.reshape((halves, group_count, -1, block.shape[2]))
        if group_count == 2:
            came = swap(take(block, 1 - my_rank, 1), "dp")
            expert_parts.append((take(block, my_rank, 1), came))
        else:
            block = lax.psum_scatter(block, "dp", scatter_dimension=1, tiled=False)
            expert_parts.append((block, None))

    logit_cot = (gates * (gate_cot - jnp.sum(gates * gate_cot, axis=1, keepdims=True))).astype(
        jnp.bfloat16
    )
    grad_router = dot_left(mid_low, logit_cot)
    shares = [share_down.send().start(rows_back), share_up.send().start(rows_back)]
    mid_cot = rows_back.astype(jnp.float32) + dot_right(logit_cot, w_router) + shared_in_cot
    middle_norm_cot, gain_two_cot = norm_two_back(mid_cot)
    middle_cot = row_cot + middle_norm_cot
    branch_cot = middle_cot.astype(jnp.bfloat16)
    block_out = (
        (valid_rows * (middle + moe_out + shared_out))
        .astype(jnp.bfloat16)
        .reshape(group_count, -1, model_width)
    )
    back_out = lax.all_to_all(block_out, "dp", split_axis=0, concat_axis=0, tiled=True)
    out_half, gate_half = model_width // 2, gate_width // 2
    outs = [
        WeightGrad(gated_low, branch_cot[:, :out_half], "e1", "dp").send().start(),
        WeightGrad(gated_low, branch_cot[:, out_half:], "dp", "e1").send().start(),
    ]
    scan_cot, gate_cot_full, gated_gain_cot = gated_back(dot_right(branch_cot, w_out))
    gate_cot_low = after(gate_cot_full.astype(jnp.bfloat16), *[grad.sent for grad in shares])
    ins = [
        WeightGrad(normed_low, gate_cot_low[:, :gate_half], "e1", "dp").send().start(),
        WeightGrad(normed_low, gate_cot_low[:, gate_half:], "dp", "e1").send().start(),
    ]
    ready = [grad.before for grad in shares + outs + ins]
    mixed_cot, kernel_cot, shift_cot, skip_cot, step_cot, decay_cot = scan_backward(
        mixed, after(scan_cot, *ready), before, *scan_args, BLK
    )
    firsts = shares + outs + ins
    mixed_cot = after(mixed_cot, moe_out, *[grad.sent for grad in outs + ins])
    half_columns = mixed_cot.shape[1] // (2 * LANES) * LANES
    lasts = [
        WeightGrad(normed_low, mixed_cot[:, :half_columns], "e1", "dp").send().start(),
        WeightGrad(normed_low, mixed_cot[:, half_columns:], "dp", "e1").send().start(),
    ]
    gone = [grad.before for grad in lasts]
    expert_sums = [
        kept if came is None else add(kept, after(came, *gone)) for kept, came in expert_parts
    ]
    expert_came = [swap(block[1], "e3") for block in expert_sums]
    for grad in firsts:
        grad.step(*gone).start()
    for grad in lasts:
        grad.step(*[block[1] for block in expert_sums]).start()
    gone = [grad.before for grad in lasts]
    flat_norm_cot, gain_one_cot = norm_one_back(
        dot_right(after(gate_cot_low, *gone), w_gate)
        + dot_right(after(mixed_cot, *gone), w_scan)
    )
    flat_norm_cot = after(flat_norm_cot, *expert_came)
    for grad in firsts:
        grad.step(*gone).start()
    for grad in lasts:
        grad.step().start()
    gone = [grad.before for grad in lasts]
    grad_expert_up, grad_expert_down = (
        add(block[0].astype(jnp.float32), after(came, *gone))[None]
        for block, came in zip(expert_sums, expert_came)
    )
    for grad in firsts:
        grad.step(*gone).start()
    sum_shared_down, sum_shared_up = (grad.finish() for grad in shares)
    sum_out = jnp.concatenate([grad.finish() for grad in outs], axis=1)
    sum_in = jnp.concatenate([grad.finish() for grad in ins + lasts], axis=1)
    sum_in = sum_in[:, : in_weight.shape[1]]
    kernel_cot, shift_cot = kernel_cot.T, shift_cot[0]
    step_cot, decay_cot = step_cot[0, :head_count], decay_cot[0, :head_count]
    skip_cot = jnp.sum(skip_cot.reshape(head_count, -1), axis=1)
    input_grad = (
        (middle_cot + flat_norm_cot).astype(jnp.bfloat16).reshape(group_count, -1, model_width)
    )
    back_grad = lax.all_to_all(input_grad, "dp", split_axis=0, concat_axis=0, tiled=True)

    heads = jnp.concatenate([step_cot, decay_cot, skip_cot])
    small_cots = [gain_one_cot, kernel_cot, shift_cot, gated_gain_cot, gain_two_cot, grad_router]
    parts = [v.reshape(device_total, -1) for v in small_cots]
    parts.append(jnp.broadcast_to(heads[None], (device_total, heads.shape[0])))
    small_came = lax.all_to_all(
        jnp.concatenate(parts, axis=1), EVERY, split_axis=0, concat_axis=0, tiled=True
    )
    small_sum = jnp.sum(after(small_came, *[grad.before for grad in lasts]), axis=0)
    sums = []
    offset = 0
    for v in small:
        sums.append(small_sum[offset : offset + v.size].reshape(v.shape))
        offset += v.size
    head_sums = small_sum[offset:].reshape(3, head_count)
    final_out = jnp.take(back_out, seq_order, axis=0)
    final_grad = jnp.take(back_grad, seq_order, axis=0)
    return (
        final_out,
        final_grad,
        sums[0],
        sum_in,
        sums[1],
        sums[2],
        head_sums[0],
        head_sums[1],
        head_sums[2],
        sums[3],
        sum_out,
        sums[4],
        sums[5],
        grad_expert_up,
        grad_expert_down,
        sum_shared_up,
        sum_shared_down,
    )


def solution(mesh):
    fine = Mesh(
        mesh.devices.reshape((mesh.shape["dp"], 2, 2, 2, mesh.shape["expert"] // 8)), EVERY
    )
    rows = P(SPLIT, "dp", None)
    flat = P(EVERY)
    split = P(EVERY, None)
    in_specs = (
        rows,
        rows,
        P(SPLIT),
        P(SPLIT),
        P(EVERY, None, None),
        flat,
        split,
        split,
        flat,
        P(),
        P(),
        P(),
        flat,
        split,
        flat,
        split,
        rows,
        rows,
        split,
        split,
    )
    out_specs = (
        rows,
        rows,
        flat,
        split,
        split,
        flat,
        P(),
        P(),
        P(),
        flat,
        split,
        flat,
        split,
        rows,
        rows,
        split,
        split,
    )
    return jax.shard_map(local, mesh=fine, in_specs=in_specs, out_specs=out_specs, check_vma=False)
```

```python
from functools import partial

import jax
import jax.numpy as jnp
from jax import lax
from jax.experimental import pallas as pl
from jax.experimental.pallas import tpu as pltpu
from jax.sharding import Mesh, PartitionSpec as P

BLK = 128
LANES = 128
INTERPRET = False
NEVER = -1e30
EPSILON = 1e-05
FULL_PRECISION = lax.Precision.HIGHEST
SPLIT = ("e3", "e2", "e1", "e0")
EVERY = ("dp",) + SPLIT
GROUP = SPLIT[1:]


def rms_scale(values, gain_row):
    return (
        values * lax.rsqrt(jnp.mean(values * values, axis=-1, keepdims=True) + EPSILON) * gain_row
    )


def swiglu(pre_act):
    half_width = pre_act.shape[-1] // 2
    return jax.nn.silu(pre_act[..., :half_width]) * pre_act[..., half_width:]


def mm(left_mat, right_mat, left_dim=1, right_dim=0):
    return lax.dot_general(
        left_mat,
        right_mat,
        (((left_dim,), (right_dim,)), ((), ())),
        preferred_element_type=jnp.float32,
    )


def mm_parts(values, ones, right_dim=0):
    high = values.astype(jnp.bfloat16)
    rest = values - high.astype(jnp.float32)
    mid = rest.astype(jnp.bfloat16)
    low = (rest - mid.astype(jnp.float32)).astype(jnp.bfloat16)
    return (
        mm(high, ones, 1, right_dim) + mm(mid, ones, 1, right_dim) + mm(low, ones, 1, right_dim)
    )


def mm_full(left_mat, right_mat):
    return lax.dot_general(
        left_mat,
        right_mat,
        (((1,), (0,)), ((), ())),
        precision=FULL_PRECISION,
        preferred_element_type=jnp.float32,
    )


def iotas(size):
    return (
        lax.broadcasted_iota(jnp.int32, (size, LANES), 0),
        lax.broadcasted_iota(jnp.int32, (size, LANES), 1),
    )


def step_terms(raw, bias, decay, spread, ran, steps, run_rows):
    size = raw.shape[0]
    down, across = iotas(size)
    shifted = raw + bias
    step = jnp.maximum(shifted, 0.0) + jnp.log1p(jnp.exp(-jnp.abs(shifted)))
    rate = -jnp.exp(decay) * step
    run = mm_full((down >= across).astype(jnp.float32), rate)
    ran[...] = mm_parts(run, spread)
    steps[...] = mm_parts(step, spread)
    run_rows[...] = run.T
    return shifted, step, rate


def conv_at(ext, taps, shift, cols, size, width):
    total = shift[:, cols]
    for tap in range(width):
        total = total + taps[tap : tap + 1, cols] * ext[pl.ds(9 - width + tap, size), cols]
    return total


def scan_kernel(
    mixed, taps, shift, bias, decay, skip, spread, y_out, before_out,
    ext, state, ran, steps, run_rows, crossed, fed,
    *, width,
):
    size = mixed.shape[0]
    inner = skip.shape[1]
    channels = shift.shape[1]
    wide = inner // LANES
    head = channels

    @pl.when(pl.program_id(0) == 0)
    def _():
        ext[pl.ds(0, 8), :] = jnp.zeros((8, channels), jnp.float32)
        state[...] = jnp.zeros_like(state)

    @pl.when(pl.program_id(0) > 0)
    def _():
        ext[pl.ds(0, 8), :] = ext[pl.ds(size, 8), :]

    ext[pl.ds(8, size), :] = mixed[:, :channels]
    step_terms(mixed[:, head:], bias[...], decay[...], spread[...], ran, steps, run_rows)
    down, across = iotas(size)
    causal = down >= across
    first = across < LANES // 2
    keep = jax.nn.silu(conv_at(ext, taps, shift, pl.ds(inner, LANES), size, width))
    read = jax.nn.silu(conv_at(ext, taps, shift, pl.ds(inner + LANES, LANES), size, width))
    read_low = read.astype(jnp.bfloat16)
    scores = mm(read_low, keep.astype(jnp.bfloat16), 1, 1)
    crossed[...] = mm(read_low, state[...].astype(jnp.bfloat16))
    before_out[0] = state[...]

    def pair(number, carry):
        cols = pl.ds(pl.multiple_of(number * LANES, LANES), LANES)
        x = jax.nn.silu(conv_at(ext, taps, shift, cols, size, width))
        run = ran[:, cols]
        stepped = x * steps[:, cols]
        stepped_low = stepped.astype(jnp.bfloat16)
        inside = []
        for one in range(2):
            at_row = jnp.broadcast_to(run[:, one * (LANES // 2)][:, None], (size, LANES))
            at_col = run_rows[pl.ds(2 * number + one, 1), :]
            mix = scores * jnp.exp(jnp.where(causal, at_row - at_col, NEVER))
            inside.append(mm(mix.astype(jnp.bfloat16), stepped_low))
        y_out[:, cols] = (
            jnp.where(first, inside[0], inside[1])
            + jnp.exp(run) * crossed[:, cols]
            + skip[:, cols] * x
        )
        fed[:, cols] = (stepped * jnp.exp(run[size - 1 :, :] - run)).astype(jnp.bfloat16)
        return carry

    lax.fori_loop(0, wide, pair, 0)
    state[...] = jnp.exp(ran[pl.ds(size - 1, 1), :]) * state[...] + mm(
        keep.T.astype(jnp.bfloat16), fed[...]
    )


def scan_back_kernel(
    mixed, halo, y_cot, before, taps, shift, bias, decay, skip, spread,
    mixed_cot, taps_cot, shift_cot, skip_cot, bias_cot, decay_cot,
    ext, cot_ext, after, ran, steps, run_rows, crossed, kept, spill, turned, fed, heard, col_rows, scores_cot, ends,
    *, width,
):
    size = mixed.shape[0]
    inner = skip.shape[1]
    channels = shift.shape[1]
    wide = inner // LANES
    head = channels
    half = LANES // 2
    started = pl.program_id(0) == 0

    @pl.when(started)
    def _():
        cot_ext[pl.ds(size, 8), :] = jnp.zeros((8, channels), jnp.float32)
        after[...] = jnp.zeros_like(after)
        taps_cot[...] = jnp.zeros_like(taps_cot)
        shift_cot[...] = jnp.zeros_like(shift_cot)
        skip_cot[...] = jnp.zeros_like(skip_cot)
        bias_cot[...] = jnp.zeros_like(bias_cot)
        decay_cot[...] = jnp.zeros_like(decay_cot)

    @pl.when(jnp.logical_not(started))
    def _():
        cot_ext[pl.ds(size, 8), :] = cot_ext[pl.ds(0, 8), :]

    top = pl.program_id(0) == pl.num_programs(0) - 1
    ext[pl.ds(0, 8), :] = jnp.where(top, 0.0, halo[:, :channels])
    ext[pl.ds(8, size), :] = mixed[:, :channels]
    shifted, step, rate = step_terms(
        mixed[:, head:], bias[...], decay[...], spread[...], ran, steps, run_rows
    )
    down, across = iotas(size)
    later = across >= down
    first = across < half
    keep_cols = pl.ds(inner, LANES)
    read_cols = pl.ds(inner + LANES, LANES)
    keep_pre = conv_at(ext, taps, shift, keep_cols, size, width)
    read_pre = conv_at(ext, taps, shift, read_cols, size, width)
    keep, read = jax.nn.silu(keep_pre), jax.nn.silu(read_pre)
    keep_low, read_low = keep.astype(jnp.bfloat16), read.astype(jnp.bfloat16)
    scores = mm(keep_low, read_low, 1, 1)
    before_low = before[0].astype(jnp.bfloat16)
    after_low = after[...].astype(jnp.bfloat16)
    crossed[...] = mm(read_low, before_low)
    kept[...] = mm(keep_low, after_low)
    scores_cot[...] = jnp.zeros_like(scores_cot)
    col_rows[...] = jnp.zeros_like(col_rows)

    def finish(cols, pre, cot):
        gate = jax.nn.sigmoid(pre)
        cot = cot * (gate * (1.0 + pre * (1.0 - gate)))
        cot_ext[pl.ds(0, size), cols] = cot
        total = None
        for tap in range(width):
            part = taps[tap : tap + 1, cols] * cot_ext[pl.ds(width - 1 - tap, size), cols]
            total = part if total is None else total + part
            taps_cot[tap : tap + 1, cols] += jnp.sum(
                cot * ext[pl.ds(9 - width + tap, size), cols], axis=0, keepdims=True
            )
        shift_cot[:, cols] += jnp.sum(cot, axis=0, keepdims=True)
        mixed_cot[:, cols] = total.astype(jnp.bfloat16)

    def pair(number, carry):
        cols = pl.ds(pl.multiple_of(number * LANES, LANES), LANES)
        pre = conv_at(ext, taps, shift, cols, size, width)
        x = jax.nn.silu(pre)
        run = ran[:, cols]
        last = run[size - 1 :, :]
        steps_here = steps[:, cols]
        stepped = x * steps_here
        fade = jnp.exp(last - run)
        reach = jnp.exp(run)
        cot = y_cot[:, cols]
        cot_low = cot.astype(jnp.bfloat16)
        from_state = kept[:, cols] * fade
        sums, inside = [], []
        for one in range(2):
            at_row = jnp.broadcast_to(run[:, one * half][:, None], (size, LANES))
            at_col = run_rows[pl.ds(2 * number + one, 1), :]
            decayed = jnp.exp(jnp.where(later, at_col - at_row, NEVER))
            mine = first if one == 0 else jnp.logical_not(first)
            mix_cot = mm(jnp.where(mine, stepped, 0.0).astype(jnp.bfloat16), cot_low, 1, 1)
            decayed_cot = mix_cot * decayed
            scores_cot[...] += decayed_cot
            moved = decayed_cot * scores
            sums.append(jnp.sum(moved, axis=1, keepdims=True))
            col_rows[pl.ds(2 * number + one, 1), :] = jnp.sum(moved, axis=0, keepdims=True)
            inside.append(mm((scores * decayed).astype(jnp.bfloat16), cot_low))
        stepped_cot = jnp.where(first, inside[0], inside[1]) + from_state
        heard_here = reach * cot
        passed = stepped * from_state
        spill[:, cols] = (
            heard_here * crossed[:, cols]
            - passed
            - jnp.where(first, sums[0], sums[1]) * (1.0 / half)
        )
        turned[:, cols] = x * stepped_cot
        ends[:, cols] = jnp.sum(passed, axis=0, keepdims=True) + jnp.exp(last) * jnp.sum(
            before[0, :, cols] * after[:, cols], axis=0, keepdims=True
        )
        skip_cot[:, cols] += jnp.sum(x * cot, axis=0, keepdims=True)
        heard[:, cols] = heard_here.astype(jnp.bfloat16)
        fed[:, cols] = (stepped * fade).astype(jnp.bfloat16)
        finish(cols, pre, steps_here * stepped_cot + skip[:, cols] * cot)
        return carry

    lax.fori_loop(0, wide, pair, 0)
    scores_cot_low = scores_cot[...].astype(jnp.bfloat16)
    scores_cot_turned = scores_cot[...].T.astype(jnp.bfloat16)
    read_cot = mm(heard[...], before_low, 1, 1) + mm(scores_cot_turned, keep_low)
    keep_cot = mm(fed[...], after_low, 1, 1) + mm(scores_cot_low, read_low)
    finish(keep_cols, keep_pre, keep_cot)
    finish(read_cols, read_pre, read_cot)
    run_cot = mm_parts(spill[...], spread[...], 1) + col_rows[...].T
    end_cot = mm_parts(jnp.broadcast_to(ends[...], (8, inner)), spread[...], 1)[0:1]
    run_cot = run_cot + jnp.where(down == size - 1, end_cot, 0.0)
    rate_cot = mm_full(later.astype(jnp.float32), run_cot)
    step_cot = mm_parts(turned[...], spread[...], 1) - jnp.exp(decay[...]) * rate_cot
    raw_cot = step_cot * jax.nn.sigmoid(shifted)
    bias_cot[...] += jnp.sum(raw_cot, axis=0, keepdims=True)
    decay_cot[...] += jnp.sum(rate_cot * rate, axis=0, keepdims=True)
    mixed_cot[:, head:] = raw_cot.astype(jnp.bfloat16)
    after[...] = jnp.exp(ran[pl.ds(size - 1, 1), :]) * after[...] + mm(
        read.T.astype(jnp.bfloat16), heard[...]
    )


def whole(shape):
    return pl.BlockSpec(shape, lambda step: (0,) * len(shape))


def head_spread(heads, inner):
    return (
        lax.broadcasted_iota(jnp.int32, (LANES, inner), 0)
        == lax.broadcasted_iota(jnp.int32, (LANES, inner), 1) // (inner // heads)
    ).astype(jnp.bfloat16)


def scan_forward(mixed, taps, shift, bias, decay, skip, spread, block_len):
    rows, total = mixed.shape
    inner = skip.shape[1]
    channels = shift.shape[1]
    blocks = rows // block_len
    state_width = (channels - inner) // 2
    f32, low = jnp.float32, jnp.bfloat16
    return pl.pallas_call(
        partial(scan_kernel, width=taps.shape[0]),
        grid=(blocks,),
        in_specs=[
            pl.BlockSpec((block_len, total), lambda step: (step, 0)),
            whole(taps.shape),
            whole(shift.shape),
            whole(bias.shape),
            whole(decay.shape),
            whole(skip.shape),
            whole(spread.shape),
        ],
        out_specs=[
            pl.BlockSpec((block_len, inner), lambda step: (step, 0)),
            pl.BlockSpec((1, state_width, inner), lambda step: (step, 0, 0)),
        ],
        out_shape=[
            jax.ShapeDtypeStruct((rows, inner), f32),
            jax.ShapeDtypeStruct((blocks, state_width, inner), f32),
        ],
        scratch_shapes=[
            pltpu.VMEM((block_len + 8, channels), f32),
            pltpu.VMEM((state_width, inner), f32),
            pltpu.VMEM((block_len, inner), f32),
            pltpu.VMEM((block_len, inner), f32),
            pltpu.VMEM((LANES, block_len), f32),
            pltpu.VMEM((block_len, inner), f32),
            pltpu.VMEM((block_len, inner), low),
        ],
        compiler_params=pltpu.CompilerParams(vmem_limit_bytes=48 << 20),
        cost_estimate=pl.CostEstimate(
            flops=10**9, transcendentals=10**7, bytes_accessed=120 * 10**6
        ),
        interpret=INTERPRET,
        name="scan_forward",
    )(mixed, taps, shift, bias, decay, skip, spread)


def scan_backward(mixed, y_cot, before, taps, shift, bias, decay, skip, spread, block_len):
    rows, total = mixed.shape
    inner = skip.shape[1]
    channels = shift.shape[1]
    blocks = rows // block_len
    state_width = (channels - inner) // 2
    f32, low = jnp.float32, jnp.bfloat16
    eighths = block_len // 8
    back = blocks - 1
    return pl.pallas_call(
        partial(scan_back_kernel, width=taps.shape[0]),
        grid=(blocks,),
        in_specs=[
            pl.BlockSpec((block_len, total), lambda step: (back - step, 0)),
            pl.BlockSpec(
                (8, total), lambda step: (jnp.maximum((back - step) * eighths - 1, 0), 0)
            ),
            pl.BlockSpec((block_len, inner), lambda step: (back - step, 0)),
            pl.BlockSpec((1, state_width, inner), lambda step: (back - step, 0, 0)),
            whole(taps.shape),
            whole(shift.shape),
            whole(bias.shape),
            whole(decay.shape),
            whole(skip.shape),
            whole(spread.shape),
        ],
        out_specs=[
            pl.BlockSpec((block_len, total), lambda step: (back - step, 0)),
            whole(taps.shape),
            whole(shift.shape),
            whole(skip.shape),
            whole(bias.shape),
            whole(decay.shape),
        ],
        out_shape=[
            jax.ShapeDtypeStruct((rows, total), low),
            jax.ShapeDtypeStruct(taps.shape, f32),
            jax.ShapeDtypeStruct(shift.shape, f32),
            jax.ShapeDtypeStruct(skip.shape, f32),
            jax.ShapeDtypeStruct(bias.shape, f32),
            jax.ShapeDtypeStruct(decay.shape, f32),
        ],
        scratch_shapes=[
            pltpu.VMEM((block_len + 8, channels), f32),
            pltpu.VMEM((block_len + 8, channels), f32),
            pltpu.VMEM((state_width, inner), f32),
            pltpu.VMEM((block_len, inner), f32),
            pltpu.VMEM((block_len, inner), f32),
            pltpu.VMEM((LANES, block_len), f32),
            pltpu.VMEM((block_len, inner), f32),
            pltpu.VMEM((block_len, inner), f32),
            pltpu.VMEM((block_len, inner), f32),
            pltpu.VMEM((block_len, inner), f32),
            pltpu.VMEM((block_len, inner), low),
            pltpu.VMEM((block_len, inner), low),
            pltpu.VMEM((LANES, block_len), f32),
            pltpu.VMEM((block_len, block_len), f32),
            pltpu.VMEM((1, inner), f32),
        ],
        compiler_params=pltpu.CompilerParams(vmem_limit_bytes=56 << 20),
        cost_estimate=pl.CostEstimate(
            flops=2 * 10**9, transcendentals=10**7, bytes_accessed=240 * 10**6
        ),
        interpret=INTERPRET,
        name="scan_backward",
    )(mixed, mixed, y_cot, before, taps, shift, bias, decay, skip, spread)


def dot_right(left_mat, right_mat):
    return lax.dot_general(
        left_mat, right_mat, (((1,), (1,)), ((), ())), preferred_element_type=jnp.float32
    )


def dot_left(left_mat, right_mat):
    return lax.dot_general(
        left_mat, right_mat, (((0,), (0,)), ((), ())), preferred_element_type=jnp.float32
    )


def to_low(weight):
    return weight.astype(jnp.bfloat16)


def gather_rows(block, axes):
    return lax.all_gather(block, axes, axis=0, tiled=True)


def tell(row, axes):
    return lax.all_to_all(
        jnp.broadcast_to(row, (lax.axis_size(axes),) + row.shape[1:]),
        axes,
        split_axis=0,
        concat_axis=0,
        tiled=True,
    )


def scatter_rows(block, axes):
    return lax.psum_scatter(block, axes, scatter_dimension=0, tiled=True)


def dot(left_mat, right_mat):
    return jnp.dot(left_mat, right_mat, preferred_element_type=jnp.float32)


def swap(block, axis):
    return lax.ppermute(block, axis, [(0, 1), (1, 0)])


def after(value, *others):
    return lax.optimization_barrier((value,) + others)[0]


def spread_rows(block, second, third, gates):
    if lax.axis_size(second) != 2:
        second, third = third, second
    whole_block = block.reshape((1,) * len(EVERY) + block.shape)
    for axis, gate in zip(("e3", "e2", third, second, "e0"), gates):
        at = EVERY.index(axis)
        if lax.axis_size(axis) == 2:
            came = swap(whole_block, axis)
            if gate is not None:
                came = after(came, gate)
            whole_block = join(whole_block, came, lax.axis_index(axis), at)
        else:
            whole_block = lax.all_gather(whole_block, axis, axis=at, tiled=True)
    return whole_block.reshape(-1, block.shape[1])


def take(block, place, axis_at):
    return lax.dynamic_index_in_dim(block, place, axis_at, keepdims=False)


def fold(block, layout, order):
    layout = list(layout)
    for axis in order:
        at = layout.index(axis)
        if lax.axis_size(axis) == 2:
            place = lax.axis_index(axis)
            came = swap(take(block, 1 - place, at), axis)
            block = add(take(block, place, at), came)
        else:
            block = lax.psum_scatter(block, axis, scatter_dimension=at, tiled=False)
        layout.pop(at)
    return block


def add(one, other):
    return (one.astype(jnp.float32) + other.astype(jnp.float32)).astype(one.dtype)


class WeightGrad:
    def __init__(self, left_mat, right_mat, second, third):
        sizes = [lax.axis_size(axis) for axis in EVERY]
        if lax.axis_size(second) != 2:
            second, third = third, second
        self.second = second
        self.order = [third, "e2", "e3"]
        self.inner = left_mat.shape[0]
        self.left_rows = left_mat.T.reshape(sizes + [-1, self.inner])
        self.right_mat = right_mat
        self.layout = [axis for axis in EVERY if axis not in ("e0", second)]
        self.one, self.two = lax.axis_index("e0"), lax.axis_index(second)
        self.far = swap(self.piece(1 - self.one, 1 - self.two).astype(jnp.bfloat16), "e0")
        self.near = swap(self.piece(1 - self.one, self.two).astype(jnp.bfloat16), "e0")

    def piece(self, place_one, place_two):
        part = take(self.left_rows, place_one, EVERY.index("e0"))
        part = take(part, place_two, EVERY.index(self.second))
        return dot(part.reshape(-1, self.inner), self.right_mat)

    def send(self):
        far = self.piece(self.one, 1 - self.two) + self.far.astype(jnp.float32)
        self.sent = far.astype(jnp.bfloat16)
        near = self.piece(self.one, self.two) + self.near.astype(jnp.float32)
        self.kept = near.astype(jnp.bfloat16)
        self.axis = self.second
        return self

    def start(self, *gates):
        self.before = self.kept if self.sent is None else self.sent
        if self.sent is not None:
            self.sent = swap(after(self.sent, *gates) if gates else self.sent, self.axis)
        return self

    def step(self, *gates):
        block = self.kept
        if self.sent is not None:
            block = add(block, after(self.sent, *gates) if gates else self.sent)
        if self.axis == self.second:
            share = self.left_rows.shape[5]
            block = block.reshape([lax.axis_size(axis) for axis in self.layout] + [share, -1])
        if not self.order:
            self.total = block.astype(jnp.float32)
            return self
        self.axis = self.order.pop(0)
        at = self.layout.index(self.axis)
        self.layout.pop(at)
        if lax.axis_size(self.axis) == 2:
            place = lax.axis_index(self.axis)
            self.kept, self.sent = take(block, place, at), take(block, 1 - place, at)
        else:
            self.kept = lax.psum_scatter(block, self.axis, scatter_dimension=at, tiled=False)
            self.sent = None
        return self

    def finish(self):
        while self.order:
            self.step().start()
        return self.step().total


def join(mine, other, place, axis_at):
    return jnp.where(
        place == 0,
        jnp.concatenate([mine, other], axis=axis_at),
        jnp.concatenate([other, mine], axis=axis_at),
    )


def gather_halves(both, gate):
    if lax.axis_size("dp") == 2:
        return join(both, after(swap(both, "dp"), gate), lax.axis_index("dp"), 1)
    return lax.all_gather(both, "dp", axis=1, tiled=True)


def local(
    tokens_in,
    out_grad,
    seq_lengths,
    seq_order,
    routes_top,
    norm_gain,
    in_weight,
    conv_weight,
    conv_bias,
    step_bias,
    decay_log,
    skip_gain,
    gated_gain,
    out_weight,
    ffn_gain,
    router_weight,
    expert_gate_up,
    expert_down,
    shared_gate_up,
    shared_down,
):
    group_count = lax.axis_size("dp")
    my_rank = lax.axis_index("dp")
    peers = lax.axis_size(GROUP)
    halves = lax.axis_size("e3")
    device_total = lax.axis_size(EVERY)

    small = [norm_gain, conv_weight, conv_bias, gated_gain, ffn_gain, router_weight]
    small_flat = jnp.concatenate([to_low(v).reshape(1, -1) for v in small], axis=1)
    small_all = tell(small_flat, EVERY)
    smalls = []
    offset = 0
    for v in small:
        smalls.append(
            small_all[:, offset : offset + v.size].reshape((device_total * v.shape[0],) + v.shape[1:])
        )
        offset += v.size
    gain_one, kernel_low, shift_low, gated_scale_low, gain_two, w_router = smalls

    slot_rows = lax.broadcasted_iota(jnp.int32, (group_count, group_count), 0)
    slot_cols = lax.broadcasted_iota(jnp.int32, (group_count, group_count), 1)
    picks = (seq_order[None, :] == slot_rows).astype(jnp.int32)
    inverse = jnp.sum(picks * slot_cols, axis=1)
    my_length = jnp.sum(jnp.where(seq_order == my_rank, seq_lengths, 0))
    dealt_in, dealt_grad = (
        lax.all_to_all(
            jnp.take(block, inverse, axis=0), "dp", split_axis=0, concat_axis=0, tiled=True
        )
        for block in (tokens_in, out_grad)
    )
    model_width = tokens_in.shape[2]
    row_count = dealt_in.shape[0] * dealt_in.shape[1]
    top_count = routes_top.shape[2]
    expert_count = w_router.shape[1]
    positions = lax.broadcasted_iota(jnp.int32, (row_count, 1), 0)
    valid = positions < my_length
    valid_rows = valid.astype(jnp.float32)
    cot_low = jnp.where(valid, dealt_grad.reshape(row_count, model_width), 0)
    row_cot = cot_low.astype(jnp.float32)

    gate_width = gated_gain.shape[0] * device_total
    head_count = step_bias.shape[0]
    pad_heads = ((0, 0), (0, LANES - head_count))
    w_scan = gather_rows(jnp.pad(to_low(in_weight[:, gate_width:]), pad_heads), EVERY)
    w_gate = gather_rows(to_low(in_weight[:, :gate_width]), EVERY)
    routes = routes_top.reshape(row_count, top_count)
    expert_ids = lax.broadcasted_iota(jnp.int32, (1, expert_count), 1)
    chosen = jnp.any(routes[:, :, None] == expert_ids[:, None, :], axis=1)
    routes_all = tell(jnp.where(valid, routes, -1)[None], GROUP)
    out_low = to_low(out_weight)
    up_low, down_low = lax.optimization_barrier(
        (to_low(expert_gate_up), to_low(expert_down), small_all, routes_all, dealt_in)
    )[:2]
    my_place = lax.axis_index(GROUP)
    mine = my_place + peers * (
        lax.axis_index("e3") ^ lax.broadcasted_iota(jnp.int32, (1, halves, 1, 1), 1)
    )
    member = jnp.any(routes_all[:, None] == mine, axis=3)
    order = (
        jnp.sum(
            (
                member[:, :, None, :]
                & (
                    lax.broadcasted_iota(jnp.int32, (row_count, row_count), 0)
                    >= lax.broadcasted_iota(jnp.int32, (row_count, row_count), 1)
                )
            ).astype(jnp.float32),
            axis=3,
        ).astype(jnp.int32)
        - 1
    )
    capacity = min(row_count, 9 * row_count * top_count // (8 * expert_count))
    capacity = -(-capacity // 32) * 32
    slot_of = jnp.where(member, order, -1)
    slot_ids = lax.broadcasted_iota(jnp.int32, (1, 1, capacity, 1), 2)
    select = (slot_of[:, :, None, :] == slot_ids).astype(jnp.bfloat16)


    w_shared_up = gather_rows(to_low(shared_gate_up), EVERY)
    w_shared_down = gather_rows(to_low(shared_down), EVERY)

    flat_in = dealt_in.reshape(row_count, model_width).astype(jnp.float32)
    normed, norm_one_back = jax.vjp(rms_scale, flat_in, gain_one.astype(jnp.float32))
    normed_low = normed.astype(jnp.bfloat16)
    normed_low = after(normed_low, slot_of)
    mixed = dot(normed_low, w_scan)
    scan_args = (
        kernel_low.astype(jnp.float32).T,
        shift_low.astype(jnp.float32)[None],
        jnp.pad(step_bias[None], pad_heads),
        jnp.pad(decay_log[None], pad_heads),
        jnp.repeat(skip_gain, gate_width // head_count)[None],
        head_spread(head_count, gate_width),
    )
    scanned, before = scan_forward(mixed, *scan_args, BLK)
    up_both = jnp.concatenate([up_low, after(swap(up_low, "e3"), mixed)], axis=0)
    down_both = jnp.concatenate([down_low, after(swap(down_low, "e3"), mixed)], axis=0)
    gate_part = dot(normed_low, w_gate)
    gated_out, gated_back = jax.vjp(
        lambda scan, gate, gain: rms_scale(scan * jax.nn.silu(gate), gain),
        scanned,
        gate_part,
        gated_scale_low.astype(jnp.float32),
    )
    gated_low = after(gated_out.astype(jnp.bfloat16), up_both, down_both)
    w_out = spread_rows(out_low, "e1", "dp", (None, None, None, scanned, gated_low))
    middle = flat_in + dot(gated_low, w_out)
    normed_two, norm_two_back = jax.vjp(rms_scale, middle, gain_two.astype(jnp.float32))
    mid_low = normed_two.astype(jnp.bfloat16)

    w_expert_up = gather_halves(up_both, mid_low)
    w_expert_down = gather_halves(down_both, mid_low)

    rows_all = gather_rows(mid_low, GROUP).reshape(peers, row_count, model_width)
    cot_all = gather_rows(after(cot_low, rows_all), GROUP).reshape(peers, row_count, model_width)
    logits = dot(mid_low, w_router)
    masked = jnp.where(chosen, logits, -jnp.inf)
    lifted = jnp.where(chosen, jnp.exp(masked - jnp.max(masked, axis=1, keepdims=True)), 0.0)
    gates = lifted / jnp.sum(lifted, axis=1, keepdims=True)
    by_peer = gates.T.reshape(halves, peers, row_count)
    by_peer = jnp.where(lax.axis_index("e3") == 0, by_peer, by_peer[::-1])
    gates_mine = lax.all_to_all(
        jnp.moveaxis(by_peer, 1, 0), GROUP, split_axis=0, concat_axis=0, tiled=True
    )
    slot_gate = jnp.sum(jnp.where(slot_of[:, :, None, :] == slot_ids, gates_mine[:, :, None, :], 0.0), axis=3)

    def pick(rows):
        return jnp.einsum(
            "sect,std->escd", select, rows, preferred_element_type=jnp.float32
        ).astype(jnp.bfloat16)

    def place(slots):
        return (
            jnp.einsum("sect,escd->std", select, slots, preferred_element_type=jnp.float32)
            .astype(jnp.bfloat16)
            .reshape(peers * row_count, model_width)
        )

    slot_gate = jnp.moveaxis(slot_gate, 1, 0)[..., None]
    expert_in = pick(rows_all)
    expert_pre = jnp.einsum(
        "escd,edf->escf", expert_in, w_expert_up, preferred_element_type=jnp.float32
    )
    expert_full, expert_back = jax.vjp(swiglu, expert_pre)
    expert_act = expert_full.astype(jnp.bfloat16)
    expert_res = jnp.einsum(
        "escf,efd->escd", expert_act, w_expert_down, preferred_element_type=jnp.float32
    ).astype(jnp.bfloat16)
    expert_cot = pick(cot_all).astype(jnp.float32)
    slot_cot = (slot_gate * expert_cot).astype(jnp.bfloat16)
    slot_gate_cot = jnp.sum(expert_cot * expert_res.astype(jnp.float32), axis=3)
    gate_cot_rows = jnp.sum(
        jnp.where(
            slot_of[:, :, None, :] == slot_ids, jnp.moveaxis(slot_gate_cot, 0, 1)[..., None], 0.0
        ),
        axis=2,
    )
    act_cot = jnp.einsum(
        "escd,efd->escf", slot_cot, w_expert_down, preferred_element_type=jnp.float32
    )
    pre_cot = expert_back(act_cot)[0].astype(jnp.bfloat16)
    input_cot = jnp.einsum(
        "escf,edf->escd", pre_cot, w_expert_up, preferred_element_type=jnp.float32
    ).astype(jnp.bfloat16)
    rows_back = scatter_rows(place(input_cot), GROUP)
    gate_cot_back = lax.all_to_all(gate_cot_rows, GROUP, split_axis=0, concat_axis=0, tiled=True)
    gate_cot = jnp.moveaxis(gate_cot_back, 2, 0)
    gate_cot = jnp.where(lax.axis_index("e3") == 0, gate_cot, gate_cot[:, :, ::-1])
    gate_cot = jnp.moveaxis(gate_cot, 2, 1).reshape(row_count, expert_count)
    moe_slots = (slot_gate * expert_res.astype(jnp.float32)).astype(jnp.bfloat16)
    moe_out = scatter_rows(after(place(moe_slots), rows_back), GROUP).astype(jnp.float32)
    grad_down_local = jnp.einsum(
        "escf,escd->efd", expert_act, slot_cot, preferred_element_type=jnp.float32
    ).astype(jnp.bfloat16)
    grad_up_local = jnp.einsum(
        "escd,escf->edf", expert_in, pre_cot, preferred_element_type=jnp.float32
    ).astype(jnp.bfloat16)
    shared_pre = dot(mid_low, w_shared_up)
    shared_full, shared_back = jax.vjp(swiglu, shared_pre)
    shared_act = shared_full.astype(jnp.bfloat16)
    shared_out = dot(shared_act, w_shared_down)
    shared_pre_cot = shared_back(dot_right(cot_low, w_shared_down))[0].astype(jnp.bfloat16)
    shared_in_cot = dot_right(shared_pre_cot, w_shared_up)

    share_down = WeightGrad(shared_act, cot_low, "dp", "e1")
    share_up = WeightGrad(mid_low, shared_pre_cot, "e1", "dp")
    expert_parts = []
    for block in (grad_up_local, grad_down_local):
        block = block.reshape((halves, group_count, -1, block.shape[2]))
        if group_count == 2:
            came = swap(take(block, 1 - my_rank, 1), "dp")
            expert_parts.append((take(block, my_rank, 1), came))
        else:
            block = lax.psum_scatter(block, "dp", scatter_dimension=1, tiled=False)
            expert_parts.append((block, None))

    logit_cot = (gates * (gate_cot - jnp.sum(gates * gate_cot, axis=1, keepdims=True))).astype(
        jnp.bfloat16
    )
    grad_router = dot_left(mid_low, logit_cot)
    shares = [share_down.send().start(rows_back), share_up.send().start(rows_back)]
    mid_cot = rows_back.astype(jnp.float32) + dot_right(logit_cot, w_router) + shared_in_cot
    middle_norm_cot, gain_two_cot = norm_two_back(mid_cot)
    middle_cot = row_cot + middle_norm_cot
    branch_cot = middle_cot.astype(jnp.bfloat16)
    block_out = (
        (valid_rows * (middle + moe_out + shared_out))
        .astype(jnp.bfloat16)
        .reshape(group_count, -1, model_width)
    )
    back_out = lax.all_to_all(block_out, "dp", split_axis=0, concat_axis=0, tiled=True)
    out_half, gate_half = model_width // 2, gate_width // 2
    outs = [
        WeightGrad(gated_low, branch_cot[:, :out_half], "e1", "dp").send().start(),
        WeightGrad(gated_low, branch_cot[:, out_half:], "dp", "e1").send().start(),
    ]
    scan_cot, gate_cot_full, gated_gain_cot = gated_back(dot_right(branch_cot, w_out))
    gate_cot_low = after(gate_cot_full.astype(jnp.bfloat16), *[grad.sent for grad in shares])
    ins = [
        WeightGrad(normed_low, gate_cot_low[:, :gate_half], "e1", "dp").send().start(),
        WeightGrad(normed_low, gate_cot_low[:, gate_half:], "dp", "e1").send().start(),
    ]
    (up_kept, up_came), down_part = expert_parts
    up_sum = up_kept if up_came is None else add(up_kept, after(up_came, scan_cot))
    up_came = swap(up_sum[1], "e3")
    ready = [grad.before for grad in shares + outs + ins] + [up_sum[1]]
    mixed_cot, kernel_cot, shift_cot, skip_cot, step_cot, decay_cot = scan_backward(
        mixed, after(scan_cot, *ready), before, *scan_args, BLK
    )
    firsts = shares + outs + ins
    mixed_cot = after(mixed_cot, moe_out, up_came, *[grad.sent for grad in outs + ins])
    half_columns = mixed_cot.shape[1] // (2 * LANES) * LANES
    lasts = [
        WeightGrad(normed_low, mixed_cot[:, :half_columns], "e1", "dp").send().start(),
        WeightGrad(normed_low, mixed_cot[:, half_columns:], "dp", "e1").send().start(),
    ]
    gone = [grad.before for grad in lasts]
    down_kept, down_came = down_part
    down_sum = down_kept if down_came is None else add(down_kept, after(down_came, *gone))
    expert_sums = [up_sum, down_sum]
    down_came = swap(down_sum[1], "e3")
    expert_came = [up_came, down_came]
    for grad in firsts:
        grad.step(*gone).start()
    for grad in lasts:
        grad.step(down_sum[1]).start()
    gone = [grad.before for grad in lasts]
    flat_norm_cot, gain_one_cot = norm_one_back(
        dot_right(after(gate_cot_low, *gone), w_gate)
        + dot_right(after(mixed_cot, *gone), w_scan)
    )
    flat_norm_cot = after(flat_norm_cot, down_came)
    for grad in firsts:
        grad.step(*gone).start()
    for grad in lasts:
        grad.step().start()
    gone = [grad.before for grad in lasts]
    grad_expert_up, grad_expert_down = (
        add(block[0].astype(jnp.float32), after(came, *gone))[None]
        for block, came in zip(expert_sums, expert_came)
    )
    for grad in firsts:
        grad.step(*gone).start()
    sum_shared_down, sum_shared_up = (grad.finish() for grad in shares)
    sum_out = jnp.concatenate([grad.finish() for grad in outs], axis=1)
    sum_in = jnp.concatenate([grad.finish() for grad in ins + lasts], axis=1)
    sum_in = sum_in[:, : in_weight.shape[1]]
    kernel_cot, shift_cot = kernel_cot.T, shift_cot[0]
    step_cot, decay_cot = step_cot[0, :head_count], decay_cot[0, :head_count]
    skip_cot = jnp.sum(skip_cot.reshape(head_count, -1), axis=1)
    input_grad = (
        (middle_cot + flat_norm_cot).astype(jnp.bfloat16).reshape(group_count, -1, model_width)
    )
    back_grad = lax.all_to_all(input_grad, "dp", split_axis=0, concat_axis=0, tiled=True)

    heads = jnp.concatenate([step_cot, decay_cot, skip_cot])
    small_cots = [gain_one_cot, kernel_cot, shift_cot, gated_gain_cot, gain_two_cot, grad_router]
    parts = [v.reshape(device_total, -1) for v in small_cots]
    parts.append(jnp.broadcast_to(heads[None], (device_total, heads.shape[0])))
    small_came = lax.all_to_all(
        jnp.concatenate(parts, axis=1), EVERY, split_axis=0, concat_axis=0, tiled=True
    )
    small_sum = jnp.sum(after(small_came, *[grad.before for grad in lasts]), axis=0)
    sums = []
    offset = 0
    for v in small:
        sums.append(small_sum[offset : offset + v.size].reshape(v.shape))
        offset += v.size
    head_sums = small_sum[offset:].reshape(3, head_count)
    final_out = jnp.take(back_out, seq_order, axis=0)
    final_grad = jnp.take(back_grad, seq_order, axis=0)
    return (
        final_out,
        final_grad,
        sums[0],
        sum_in,
        sums[1],
        sums[2],
        head_sums[0],
        head_sums[1],
        head_sums[2],
        sums[3],
        sum_out,
        sums[4],
        sums[5],
        grad_expert_up,
        grad_expert_down,
        sum_shared_up,
        sum_shared_down,
    )


def solution(mesh):
    fine = Mesh(
        mesh.devices.reshape((mesh.shape["dp"], 2, 2, 2, mesh.shape["expert"] // 8)), EVERY
    )
    rows = P(SPLIT, "dp", None)
    flat = P(EVERY)
    split = P(EVERY, None)
    in_specs = (
        rows,
        rows,
        P(SPLIT),
        P(SPLIT),
        P(EVERY, None, None),
        flat,
        split,
        split,
        flat,
        P(),
        P(),
        P(),
        flat,
        split,
        flat,
        split,
        rows,
        rows,
        split,
        split,
    )
    out_specs = (
        rows,
        rows,
        flat,
        split,
        split,
        flat,
        P(),
        P(),
        P(),
        flat,
        split,
        flat,
        split,
        rows,
        rows,
        split,
        split,
    )
    return jax.shard_map(local, mesh=fine, in_specs=in_specs, out_specs=out_specs, check_vma=False)
```
